32 devices in a mesh: row: 8 (over y, x, core), col: 4 (over z).
Axes of the slice: x: 2, y: 2, z: 4, core: 2. Of those that a mesh axis runs over, the one named last changes fastest.
Arguments:
- transitions: bfloat16 [4, 1024, 32768], P(None, 'row', 'col'), may hold values from 1.5199184e-06 to 0.00015258789
- values: bfloat16 [32768, 6144], P('row', 'col'), may hold values from -1280 to 1280
- earlier_sum: bfloat16 [4, 1024, 6144], P(None, 'row', 'col'), may hold values from -8 to 8
- section_costs: bfloat16 [4, 1024, 6144], P(None, 'row', 'col'), may hold values from 0 to 3
Outputs:
- backed_up: float32 [1024, 6144], P('row', 'col')
The draws below stay inside these ranges and needn't reach their ends.
All inputs are finite; a program needn't handle non-finite values.
Results may differ from the reference program's by a relative error of at most 0.0003.
Values may be sent and summed in bfloat16 or wider, within the bound.
A program may use at most 192 MiB of HBM per device.

```python
import math
import jax
import jax.numpy as jnp
from jax import lax

S = 32768
A = 4
STEPS = 4
ROWS_DEV = 128
ROWS = 1024
M = 6144
N_ROW = 8


def levels(key, shape, cuts, least, largest):
    loudness = 1.0
    for axis_at, parts in cuts:
        steps = jax.random.uniform(jax.random.fold_in(jax.random.fold_in(key, 6), axis_at), (parts,), jnp.float32, least / len(cuts), largest / len(cuts))
        loudness = loudness * jnp.repeat(jnp.exp(steps), shape[axis_at] // parts).reshape((-1,) + (1,) * (len(shape) - 1 - axis_at))
    return loudness


def normal_values(own_key, extent, spread, reach, shards=(), held_as=jnp.bfloat16):
    entries = spread * jax.random.normal(own_key, extent, jnp.float32)
    if shards:
        entries = entries * levels(own_key, extent, shards, -0.22, 0.18)
    return jnp.clip(entries, -reach, reach).astype(held_as)


def setup_inputs(seed: int = 0) -> dict:
    arg_keys = jax.random.split(jax.random.key(seed), 5)
    return {
        "transitions": jnp.clip(jnp.exp(math.log(0.00015258789) - 4.609084 * jax.random.uniform(arg_keys[0], (A, ROWS, S), jnp.float32) ** levels(arg_keys[0], (A, ROWS, S), ((1, 8), (2, 4)), -0.2, 0.2)), 1.519918441772461e-06, 0.00015258789).astype(jnp.bfloat16),
        "values": normal_values(arg_keys[1], (S, M), (0.6 * S / (STEPS * S // 16) ** 0.5), 1280.0, ((0, 8), (1, 4))),
        "earlier_sum": normal_values(arg_keys[2], (A, ROWS, M), 1.5, 8.0, ((1, 8), (2, 4))),
        "section_costs": jnp.clip(3.0 * jax.random.uniform(arg_keys[3], (A, ROWS, M), jnp.float32) ** levels(arg_keys[3], (A, ROWS, M), ((1, 8), (2, 4)), -0.2, 0.2), 0.0, 3.0).astype(jnp.bfloat16),
    }


DISCOUNT = 0.97


def window_rows(transitions, values, index):
    block_width = S // N_ROW
    rows = lax.dynamic_slice_in_dim(transitions, index * ROWS_DEV, ROWS_DEV, 1)
    total = jnp.zeros((A, ROWS_DEV, values.shape[1]), jnp.float32)
    for section in range(STEPS):
        column_block = ((index + section) % N_ROW).astype(jnp.int32)
        chosen = lax.dynamic_slice_in_dim(rows, column_block * block_width, block_width, 2).astype(jnp.float32)
        states = lax.dynamic_slice_in_dim(values, column_block * block_width, block_width, 0).astype(jnp.float32)
        total = total + jnp.einsum("ars,sm->arm", chosen, states, precision=lax.Precision.HIGHEST)
    return total


def reference(transitions, values, earlier_sum, section_costs):
    indices = jnp.arange(N_ROW, dtype=jnp.int32)
    sums = lax.map(lambda index: window_rows(transitions, values, index), indices)
    window_sum = jnp.transpose(sums, (1, 0, 2, 3)).reshape(A, ROWS_DEV * N_ROW, values.shape[1])
    backup = earlier_sum.astype(jnp.float32) + window_sum
    return jnp.min(section_costs.astype(jnp.float32) + DISCOUNT * backup, axis=0)
```

```python
import functools

import jax
import jax.numpy as jnp
from jax import lax
from jax.experimental import pallas as pl
from jax.experimental.pallas import tpu as pltpu
from jax.sharding import PartitionSpec as P

STEPS = 4
PIECES = 8
DISCOUNT = 0.97
MESH = pl.DeviceIdType.MESH


def general_kernel(
    rows, cols, t_ref, v_ref, e_ref, c_ref, out_ref,
    slots, v_buf, work, arrived, e_buf, c_buf,
    in_sem, own_sem, slot_sem, first_sem, up_sem, down_sem, sum_send, sum_recv,
):
    b = lax.axis_index("row")
    z = lax.axis_index("col")
    ratio = rows // cols
    q = b // ratio
    actions = t_ref.shape[0]
    width = v_ref.shape[0]
    half = width // PIECES
    sums = (STEPS - 1) * actions
    total = STEPS * actions

    loads = [
        pltpu.make_async_copy(v_ref, v_buf, in_sem.at[0]),
        pltpu.make_async_copy(e_ref, e_buf, in_sem.at[1]),
        pltpu.make_async_copy(c_ref, c_buf, in_sem.at[2]),
    ]
    for load in loads:
        load.start()

    barrier = pltpu.get_barrier_semaphore()
    for d in range(1, STEPS):
        for by in (d, rows - d):
            pl.semaphore_signal(barrier, inc=1, device_id=((b + by) % rows, z), device_id_type=MESH)

    @pl.when(z > 0)
    def _():
        pl.semaphore_signal(barrier, inc=1, device_id=(b, z - 1), device_id_type=MESH)

    @pl.when(z < cols - 1)
    def _():
        pl.semaphore_signal(barrier, inc=1, device_id=(b, z + 1), device_id_type=MESH)

    beside = jnp.where(z > 0, 1, 0) + jnp.where(z < cols - 1, 1, 0)
    pl.semaphore_wait(barrier, 2 * (STEPS - 1) + beside)

    def held(j, a, h):
        offset = pl.multiple_of(j * width + h * half, 128)
        return t_ref.at[a, :, pl.ds(offset, half)]

    def first_copy(j, d, a, h):
        i = (d - 1) * actions + a
        return pltpu.make_async_remote_copy(
            src_ref=held(j, a, h), dst_ref=slots.at[i, h],
            send_sem=first_sem.at[j, a, h], recv_sem=slot_sem.at[i, h],
            device_id=(z * ratio + j, z), device_id_type=MESH,
        )

    def own_copy(j, a, h):
        i = (STEPS - 1) * actions + a
        return pltpu.make_async_copy(held(j, a, h), slots.at[i, h], own_sem.at[a, h])

    def for_blocks(away, own):
        for j in range(ratio):
            d = (z * ratio + j - b + rows) % rows

            @pl.when((d > 0) & (d < STEPS))
            def _():
                @pl.loop(0, actions)
                def _(a):
                    for h in range(PIECES):
                        away(j, d, a, h)

            if own is not None:
                @pl.when(d == 0)
                def _():
                    @pl.loop(0, actions)
                    def _(a):
                        for h in range(PIECES):
                            own(j, a, h)

    for_blocks(
        lambda j, d, a, h: first_copy(j, d, a, h).start(),
        lambda j, a, h: own_copy(j, a, h).start(),
    )

    def along(i, h, by, sem):
        return pltpu.make_async_remote_copy(
            src_ref=slots.at[i, h], dst_ref=slots.at[i, h],
            send_sem=sem.at[i, h], recv_sem=slot_sem.at[i, h],
            device_id=(b, z + by), device_id_type=MESH,
        )

    goes_up = (z >= q) & (z < cols - 1)
    goes_down = (z <= q) & (z > 0)

    def sum_copy(i):
        d = i // actions + 1
        return pltpu.make_async_remote_copy(
            src_ref=work.at[i], dst_ref=arrived.at[i],
            send_sem=sum_send.at[i], recv_sem=sum_recv.at[i],
            device_id=((b - d + rows) % rows, z), device_id_type=MESH,
        )

    def finish(a):
        for d in range(STEPS - 1):
            sum_copy(d * actions + a).wait_recv()

        @pl.loop(0, out_ref.shape[0] // 16)
        def _(k):
            at = pl.ds(pl.multiple_of(k * 16, 16), 16)
            backup = e_buf[a, at, :].astype(jnp.float32) + work[sums + a, at, :]
            for d in range(STEPS - 1):
                backup = backup + arrived[d * actions + a, at, :]
            cost = c_buf[a, at, :].astype(jnp.float32) + DISCOUNT * backup

            @pl.when(a == 0)
            def _():
                out_ref[at, :] = cost

            @pl.when(a > 0)
            def _():
                out_ref[at, :] = jnp.minimum(out_ref[at, :], cost)

    @pl.loop(0, total)
    def _(i):
        for h in range(PIECES):
            local = (i >= sums) & (z == q)

            @pl.when(local)
            def _():
                own_copy(b % ratio, i % actions, h).wait()

            @pl.when(jnp.logical_not(local))
            def _():
                along(i, h, 0, up_sem).wait_recv()

            @pl.when(goes_up)
            def _():
                along(i, h, 1, up_sem).start()

            @pl.when(goes_down)
            def _():
                along(i, h, -1, down_sem).start()

            if h == 0:
                @pl.when(i == 0)
                def _():
                    for load in loads:
                        load.wait()

            tile = 512

            @pl.loop(0, work.shape[2] // tile)
            def _(n):
                at = pl.ds(pl.multiple_of(n * tile, tile), tile)
                product = jnp.dot(
                    slots[i, h], v_buf[h * half:(h + 1) * half, at],
                    preferred_element_type=jnp.float32,
                )
                if h == 0:
                    work[i, :, at] = product
                else:
                    work[i, :, at] += product

        @pl.when((i >= 1) & (i <= sums))
        def _():
            sum_copy(i - 1).start()

        @pl.when(i > sums)
        def _():
            finish(i - 1 - sums)

    finish(actions - 1)

    @pl.loop(0, sums)
    def _(i):
        sum_copy(i).wait_send()

    for_blocks(lambda j, d, a, h: first_copy(j, d, a, h).wait_send(), None)

    @pl.when(goes_up)
    def _():
        @pl.loop(0, total)
        def _(i):
            for h in range(PIECES):
                along(i, h, 1, up_sem).wait_send()

    @pl.when(goes_down)
    def _():
        @pl.loop(0, total)
        def _(i):
            for h in range(PIECES):
                along(i, h, -1, down_sem).wait_send()


def general(transitions, values, earlier_sum, section_costs):
    rows = lax.axis_size("row")
    cols = lax.axis_size("col")
    actions, height, _ = transitions.shape
    width, scenarios = values.shape
    total = STEPS * actions
    sums = (STEPS - 1) * actions
    ratio = rows // cols
    anywhere = pl.BlockSpec(memory_space=pl.ANY)
    dma = pltpu.SemaphoreType.DMA
    return pl.pallas_call(
        functools.partial(general_kernel, rows, cols),
        out_shape=jax.ShapeDtypeStruct((height, scenarios), jnp.float32),
        in_specs=[anywhere] * 4,
        out_specs=pl.BlockSpec(memory_space=pltpu.VMEM),
        scratch_shapes=[
            pltpu.VMEM((total, PIECES, height, width // PIECES), jnp.bfloat16),
            pltpu.VMEM((width, scenarios), jnp.bfloat16),
            pltpu.VMEM((total, height, scenarios), jnp.float32),
            pltpu.VMEM((sums, height, scenarios), jnp.float32),
            pltpu.VMEM((actions, height, scenarios), jnp.bfloat16),
            pltpu.VMEM((actions, height, scenarios), jnp.bfloat16),
            dma((3,)),
            dma((actions, PIECES)),
            dma((total, PIECES)),
            dma((ratio, actions, PIECES)),
            dma((total, PIECES)),
            dma((total, PIECES)),
            dma((sums,)),
            dma((sums,)),
        ],
        compiler_params=pltpu.CompilerParams(
            collective_id=0, has_side_effects=True, vmem_limit_bytes=66_000_000
        ),
    )(transitions, values, earlier_sum, section_costs)


CHUNK = 256
ACROSS = (
    ((2, 0), (1, 1)), ((2, 0), (0, 1)), ((3, 0), (2, 1)), ((3, 0), (1, 1)), ((3, 0), (0, 1)),
    ((5, 3), (4, 2)), ((4, 3), (6, 2)), ((5, 3), (7, 2)),
    ((0, 3), (5, 2)), ((1, 3), (4, 2)), ((2, 3), (7, 2)), ((3, 3), (6, 2)),
    ((4, 0), (1, 1)), ((5, 0), (0, 1)), ((6, 0), (3, 1)), ((7, 0), (2, 1)),
)


def routed_kernel(
    t_ref, v_ref, e_ref, c_ref, out_ref, relay,
    slots, v_buf, acc, arr, e_buf, c_buf,
    in_sem, slot_sem, relay_sem, first_sem, direct_sem, alt_sem, fwd_sem, minor_sem, disp_sem,
    relay_z_sem, relay_in_sem, relay_x_sem, sum_send, sum_recv, there_sem,
):
    b = lax.axis_index("row")
    z = lax.axis_index("col")
    rows = 8
    k = b // 2
    odd = b % 2
    actions, height, _ = t_ref.shape
    width, scenarios = v_ref.shape
    pieces = width // CHUNK
    half = pieces // 2

    loads = [
        pltpu.make_async_copy(v_ref, v_buf, in_sem.at[0]),
        pltpu.make_async_copy(e_ref, e_buf, in_sem.at[1]),
        pltpu.make_async_copy(c_ref, c_buf, in_sem.at[2]),
    ]
    for load in loads:
        load.start()

    barrier = pltpu.get_barrier_semaphore()
    for by in range(1, rows):
        pl.semaphore_signal(barrier, inc=1, device_id=((b + by) % rows, z), device_id_type=MESH)

    @pl.when(z > 0)
    def _():
        pl.semaphore_signal(barrier, inc=1, device_id=(b, z - 1), device_id_type=MESH)

    @pl.when(z < 3)
    def _():
        pl.semaphore_signal(barrier, inc=1, device_id=(b, z + 1), device_id_type=MESH)

    greeted = rows - 1 + jnp.where(z > 0, 1, 0) + jnp.where(z < 3, 1, 0)
    for (to, by) in ACROSS:
        @pl.when((b == to[0]) & (z == to[1]))
        def _():
            pl.semaphore_signal(barrier, inc=1, device_id=by, device_id_type=MESH)

        greeted = greeted + jnp.where((b == by[0]) & (z == by[1]), 1, 0)
    pl.semaphore_wait(barrier, greeted)

    def remote(src, dst, send, recv, to):
        return pltpu.make_async_remote_copy(
            src_ref=src, dst_ref=dst, send_sem=send, recv_sem=recv, device_id=to, device_id_type=MESH
        )

    side = jnp.where(z < 2, 1, -1)

    def held(j, h):
        return t_ref.at[:, :, pl.ds(pl.multiple_of(j * width + h * CHUNK, 128), CHUNK)]

    def own_copy(j, h):
        return pltpu.make_async_copy(held(j, h), slots.at[0, h], slot_sem.at[0, h])

    def first_copy(j, d, h):
        return remote(held(j, h), slots.at[d, h], first_sem.at[j, h], slot_sem.at[d, h], (2 * z + j, z))

    def direct_copy(j, d, h):
        to = jnp.where(z == 1, 0, 3)
        return remote(held(j, h), slots.at[d, h], direct_sem.at[j, h], slot_sem.at[d, h], (2 * z + j, to))

    def far_copy(h):
        return remote(held(0, h), relay.at[0, h], alt_sem.at[0, h], relay_sem.at[0, h], (b, z + side))

    def aside_copy(h):
        return remote(held(1, h), relay.at[0, h], alt_sem.at[1, h], relay_sem.at[0, h], ((b + 3) % rows, z))

    dist = [(2 * z + j - b + rows) % rows for j in range(2)]
    is_far = dist[0] == 3
    is_aside = dist[1] == 0

    def sends_cross(j):
        return (z == 1) & (dist[j] > j) & (dist[j] <= 2 + j)

    def sends_near(j):
        return ((z == 1) | (z == 2)) & (dist[j] <= j)

    far_later = is_far & (z % 2 == 0)
    later = (z == 2) & (dist[0] == 1)

    @pl.loop(0, pieces)
    def _(h):
        for j in range(2):
            @pl.when(dist[j] == 0)
            def _():
                own_copy(j, h).start()

            @pl.when((dist[j] > 0) & (dist[j] <= 2 + j) & jnp.logical_not(later))
            def _():
                first_copy(j, dist[j], h).start()

        @pl.when(is_far)
        def _():
            far_copy(h).start()

        @pl.when(is_far & jnp.logical_not(far_later))
        def _():
            first_copy(0, 3, h).start()

        @pl.when(is_aside)
        def _():
            aside_copy(h).start()

    @pl.loop(0, STEPS)
    def _(d):
        @pl.loop(0, actions)
        def _(a):
            acc[d, a] = jnp.zeros(acc.shape[2:], jnp.float32)

    way = jnp.where(k < 2, 1, -1)
    chained = (k < 2) & (z >= k) & (z < 3) | (k >= 2) & (z <= k) & (z > 0)
    turns = (odd == 0) & (z == k) & ((k == 1) | (k == 2))
    crosses = (z == 2) & (k == 2)

    def chain_copy(d, h):
        return remote(slots.at[d, h], slots.at[d, h], fwd_sem.at[d, h], slot_sem.at[d, h], (b, z + way))

    def in_chain(d):
        return chained & (d < 3 + odd) & (d >= odd)

    def turn_copy(h):
        return remote(slots.at[3, h], slots.at[3, h], minor_sem.at[h], slot_sem.at[3, h], (b, z - way))

    def cross_copy(x, h):
        return remote(
            slots.at[1 + odd + x, h], relay.at[1 + x, h], disp_sem.at[x, h], relay_sem.at[1 + x, h], (b + 2, z)
        )

    def is_cross(d):
        return crosses & (d > odd) & (d <= 2 + odd)

    kr = (b // 2 + 2) % 4
    br = jnp.where(odd == 1, (b + 3) % rows, (b + 5) % rows)
    dr = jnp.where(odd == 1, 3, 0)
    way_r = jnp.where(kr < 2, 1, -1)
    relays = (kr < 2) & (z >= kr) | (kr >= 2) & (z <= kr)
    takes = relays & ((z != kr) | (odd == 0)) & (z + way_r >= 0) & (z + way_r <= 3)
    ends = takes & ((z + way_r == 0) | (z + way_r == 3))
    passes = takes & jnp.logical_not(ends)
    hands = takes & (z != kr)
    lifts = (z == 2) & (k == 3)

    def pass_copy(h):
        return remote(relay.at[0, h], relay.at[0, h], relay_z_sem.at[h], relay_sem.at[0, h], (b, z + way_r))

    def end_copy(h):
        return remote(
            relay.at[0, h], slots.at[dr, h], relay_z_sem.at[h], slot_sem.at[dr, h], (br, z + way_r)
        )

    def hand_copy(h):
        return remote(relay.at[0, h], slots.at[dr, h], relay_in_sem.at[h], slot_sem.at[dr, h], (br, z))

    def lift_copy(x, h):
        d = 1 + odd + x
        return remote(relay.at[1 + x, h], slots.at[d, h], relay_x_sem.at[x, h], slot_sem.at[d, h], ((b + 6) % rows, 3))

    def relay_step(h):
        pltpu.make_async_copy(relay.at[0, h], relay.at[0, h], relay_sem.at[0, h]).wait()

        @pl.when(passes)
        def _():
            pass_copy(h).start()

        @pl.when(hands)
        def _():
            hand_copy(h).start()

    def process(d, h):
        pltpu.make_async_copy(slots.at[d, h], slots.at[d, h], slot_sem.at[d, h]).wait()

        @pl.when(in_chain(d))
        def _():
            chain_copy(d, h).start()

        @pl.when(turns & (d == 3))
        def _():
            turn_copy(h).start()

        @pl.when(is_cross(d))
        def _():
            cross_copy(d - 1 - odd, h).start()

        tile = 512

        @pl.loop(0, scenarios // tile)
        def _(n):
            at = pl.ds(pl.multiple_of(n * tile, tile), tile)
            rows_at = pl.ds(pl.multiple_of(h * CHUNK, CHUNK), CHUNK)
            product = jnp.dot(
                slots[d, h].reshape(actions * height, CHUNK), v_buf[rows_at, at],
                preferred_element_type=jnp.float32,
            )
            acc[d, :, :, at] += product.reshape(actions, height, tile)

    def sum_copy(d, a):
        slot = jnp.where(odd == 1, jnp.where(d == 1, 2, 3 - d), jnp.where(d == 1, 2, 3))
        to = jnp.where(odd == 1, b - 1, (b - d + rows) % rows)
        return remote(acc.at[d, a], arr.at[slot, a], sum_send.at[d, a], sum_recv.at[slot, a], (to, z))

    def arrived(slot, a):
        pltpu.make_async_copy(arr.at[slot, a], arr.at[slot, a], sum_recv.at[slot, a]).wait()

    def send_sum(d):
        @pl.loop(0, actions)
        def _(a):
            sum_copy(d, a).start()

    def add_and_send(d):
        @pl.loop(0, actions)
        def _(a):
            arrived(2 - d, a)
            acc[d, a] += arr[2 - d, a]
            sum_copy(d, a).start()

    for load in loads:
        load.wait()

    in_turn = (k == 2) | (k == 1) & (z == 0)
    hops = jnp.where(z > k, z - k, k - z)
    far_from = jnp.where(hops == 0, jnp.where(k % 2 == 0, 17, 0), jnp.where(hops == 3, 6, 1 + 2 * hops))
    far_from = jnp.where((z == 0) & (b == 4) | (z == 3) & (b == 2), 7, jnp.where((z == 3) & (b == 4), 19, far_from))
    far_each = jnp.where(far_from >= 14, 4, 2)
    far_end = far_from + pieces // far_each
    hops_r = jnp.where(z > kr, z - kr, kr - z)
    relay_from = jnp.where(odd == 1, 2 * hops_r - 2, 4 + 2 * hops_r)
    end_from = jnp.where(odd == 1, jnp.where((kr == 0) | (kr == 3), 6, 4), jnp.where((kr == 0) | (kr == 3), 12, jnp.where(kr == 1, 18, 17)))

    @pl.loop(0, 2 * pieces)
    def _(g):
        for j in range(2):
            @pl.when(sends_cross(j) & (g // half == 2 + j - dist[j]))
            def _():
                for i in range(2):
                    direct_copy(j, dist[j], 2 * (g % half) + i).start()

            @pl.when(sends_near(j) & (g % 3 < 2) & (2 * (g // 3) + g % 3 < pieces))
            def _():
                direct_copy(j, dist[j], 2 * (g // 3) + g % 3).start()

        @pl.when(later & (g == 6))
        def _():
            @pl.loop(0, pieces)
            def _(h):
                for j in range(2):
                    first_copy(j, 1 + j, h).start()

        @pl.when(lifts & (g < pieces + 1) & (g != half))
        def _():
            for i in range(2):
                x, h = jnp.where(g < half, 1, 0), 2 * jnp.where(g < half, g, g - half - 1) + i
                pltpu.make_async_copy(relay.at[1 + x, h], relay.at[1 + x, h], relay_sem.at[1 + x, h]).wait()
                lift_copy(x, h).start()

        @pl.when(far_later & (g == 13))
        def _():
            @pl.loop(0, pieces)
            def _(h):
                first_copy(0, 3, h).start()

        @pl.loop(0, 7)
        def _(i):
            cross = g < pieces
            far_due = (g >= far_from) & (g < far_end) & (odd == 0) & (i < 3 + far_each)
            d = jnp.where(i >= 3, 3, jnp.where(i == 2, odd, 2 + odd - jnp.where(in_turn, g // half, i)))
            h = jnp.where(i >= 3, far_each * (g - far_from) + i - 3, jnp.where(in_turn, 2 * (g % half) + i, g))
            h = jnp.where(i == 2, jnp.where(cross, g // 8, g - pieces + 2), h)
            near = jnp.where(cross, g % 8 == 7, g < 2 * pieces - 2)

            @pl.when(jnp.where(i < 2, cross, jnp.where(i == 2, near, far_due)))
            def _():
                process(d, h)

        @pl.when(takes & (g >= relay_from) & (g < relay_from + half))
        def _():
            for i in range(2):
                relay_step(2 * (g - relay_from) + i)

        @pl.when(ends & (g >= end_from) & (g < end_from + 4))
        def _():
            @pl.loop(0, pieces // 4)
            def _(i):
                end_copy(pieces // 4 * (g - end_from) + i).start()

        first_at = jnp.where(in_turn & (z != 2), half, pieces)

        @pl.when((odd == 1) & (g == first_at - 1))
        def _():
            send_sum(3)

        @pl.when((odd == 1) & (g == pieces - 1))
        def _():
            send_sum(2)

        @pl.when((z == 3) & (k == 2) & (g == pieces - 1))
        def _():
            pl.semaphore_signal(there_sem, inc=1, device_id=(6, 3), device_id_type=MESH)

        @pl.when((z == 3) & (b == 6) & (g == pieces + 1))
        def _():
            pl.semaphore_wait(there_sem, 2)

        @pl.when((odd == 0) & (g == first_at + 1))
        def _():
            add_and_send(2)

        @pl.when((odd == 0) & (g == pieces + 2))
        def _():
            add_and_send(1)

        @pl.when((odd == 0) & (g == far_end - 1))
        def _():
            send_sum(3)

    @pl.when(odd == 1)
    def _():
        send_sum(1)

        @pl.loop(0, pieces)
        def _(s):
            process(0, s)

    @pl.loop(0, actions)
    def _(a):
        arrived(2, a)
        arrived(3, a)

        @pl.loop(0, height // 16)
        def _(n):
            at = pl.ds(pl.multiple_of(n * 16, 16), 16)
            backup = e_buf[a, at, :].astype(jnp.float32) + acc[0, a, at, :] + arr[2, a, at, :] + arr[3, a, at, :]
            cost = c_buf[a, at, :].astype(jnp.float32) + DISCOUNT * backup

            @pl.when(a == 0)
            def _():
                out_ref[at, :] = cost

            @pl.when(a > 0)
            def _():
                out_ref[at, :] = jnp.minimum(out_ref[at, :], cost)

    @pl.loop(1, STEPS)
    def _(d):
        @pl.loop(0, actions)
        def _(a):
            sum_copy(d, a).wait_send()

    @pl.loop(0, pieces)
    def _(h):
        for j in range(2):
            @pl.when((dist[j] > 0) & (dist[j] < STEPS))
            def _():
                first_copy(j, dist[j], h).wait_send()

            @pl.when(sends_cross(j) | sends_near(j))
            def _():
                direct_copy(j, dist[j], h).wait_send()

        @pl.when(is_far)
        def _():
            far_copy(h).wait_send()

        @pl.when(is_aside)
        def _():
            aside_copy(h).wait_send()

        @pl.loop(0, STEPS)
        def _(d):
            @pl.when(in_chain(d))
            def _():
                chain_copy(d, h).wait_send()

        @pl.when(turns)
        def _():
            turn_copy(h).wait_send()

        @pl.when(crosses)
        def _():
            for x in range(2):
                cross_copy(x, h).wait_send()

        @pl.when(passes)
        def _():
            pass_copy(h).wait_send()

        @pl.when(ends)
        def _():
            end_copy(h).wait_send()

        @pl.when(hands)
        def _():
            hand_copy(h).wait_send()

        @pl.when(lifts)
        def _():
            for x in range(2):
                lift_copy(x, h).wait_send()


def routed(transitions, values, earlier_sum, section_costs):
    actions, height, _ = transitions.shape
    width, scenarios = values.shape
    pieces = width // CHUNK
    anywhere = pl.BlockSpec(memory_space=pl.ANY)
    dma = pltpu.SemaphoreType.DMA
    return pl.pallas_call(
        routed_kernel,
        out_shape=(
            jax.ShapeDtypeStruct((height, scenarios), jnp.float32),
            jax.ShapeDtypeStruct((3, pieces, actions, height, CHUNK), jnp.bfloat16),
        ),
        in_specs=[anywhere] * 4,
        out_specs=(pl.BlockSpec(memory_space=pltpu.VMEM), anywhere),
        scratch_shapes=[
            pltpu.VMEM((STEPS, pieces, actions, height, CHUNK), jnp.bfloat16),
            pltpu.VMEM((width, scenarios), jnp.bfloat16),
            pltpu.VMEM((STEPS, actions, height, scenarios), jnp.float32),
            pltpu.VMEM((STEPS, actions, height, scenarios), jnp.float32),
            pltpu.VMEM((actions, height, scenarios), jnp.bfloat16),
            pltpu.VMEM((actions, height, scenarios), jnp.bfloat16),
            dma((3,)),
            dma((STEPS, pieces)),
            dma((3, pieces)),
            dma((2, pieces)),
            dma((2, pieces)),
            dma((2, pieces)),
            dma((STEPS, pieces)),
            dma((pieces,)),
            dma((2, pieces)),
            dma((pieces,)),
            dma((pieces,)),
            dma((2, pieces)),
            dma((STEPS, actions)),
            dma((STEPS, actions)),
            pltpu.SemaphoreType.REGULAR,
        ],
        compiler_params=pltpu.CompilerParams(
            collective_id=0, has_side_effects=True, vmem_limit_bytes=66_000_000
        ),
    )(transitions, values, earlier_sum, section_costs)[0]


def local(transitions, values, earlier_sum, section_costs):
    if lax.axis_size("row") == 8 and lax.axis_size("col") == 4:
        return routed(transitions, values, earlier_sum, section_costs)
    return general(transitions, values, earlier_sum, section_costs)


def solution(mesh):
    in_specs = (
        P(None, "row", "col"),
        P("row", "col"),
        P(None, "row", "col"),
        P(None, "row", "col"),
    )
    out_specs = P("row", "col")
    return jax.shard_map(local, mesh=mesh, in_specs=in_specs, out_specs=out_specs, check_vma=False)
```

```python
import functools

import jax
import jax.numpy as jnp
from jax import lax
from jax.experimental import pallas as pl
from jax.experimental.pallas import tpu as pltpu
from jax.sharding import PartitionSpec as P

STEPS = 4
PIECES = 8
DISCOUNT = 0.97
MESH = pl.DeviceIdType.MESH


def general_kernel(
    rows, cols, t_ref, v_ref, e_ref, c_ref, out_ref,
    slots, v_buf, work, arrived, e_buf, c_buf,
    in_sem, own_sem, slot_sem, first_sem, up_sem, down_sem, sum_send, sum_recv,
):
    b = lax.axis_index("row")
    z = lax.axis_index("col")
    ratio = rows // cols
    q = b // ratio
    actions = t_ref.shape[0]
    width = v_ref.shape[0]
    half = width // PIECES
    sums = (STEPS - 1) * actions
    total = STEPS * actions

    loads = [
        pltpu.make_async_copy(v_ref, v_buf, in_sem.at[0]),
        pltpu.make_async_copy(e_ref, e_buf, in_sem.at[1]),
        pltpu.make_async_copy(c_ref, c_buf, in_sem.at[2]),
    ]
    for load in loads:
        load.start()

    barrier = pltpu.get_barrier_semaphore()
    for d in range(1, STEPS):
        for by in (d, rows - d):
            pl.semaphore_signal(barrier, inc=1, device_id=((b + by) % rows, z), device_id_type=MESH)

    @pl.when(z > 0)
    def _():
        pl.semaphore_signal(barrier, inc=1, device_id=(b, z - 1), device_id_type=MESH)

    @pl.when(z < cols - 1)
    def _():
        pl.semaphore_signal(barrier, inc=1, device_id=(b, z + 1), device_id_type=MESH)

    beside = jnp.where(z > 0, 1, 0) + jnp.where(z < cols - 1, 1, 0)
    pl.semaphore_wait(barrier, 2 * (STEPS - 1) + beside)

    def held(j, a, h):
        offset = pl.multiple_of(j * width + h * half, 128)
        return t_ref.at[a, :, pl.ds(offset, half)]

    def first_copy(j, d, a, h):
        i = (d - 1) * actions + a
        return pltpu.make_async_remote_copy(
            src_ref=held(j, a, h), dst_ref=slots.at[i, h],
            send_sem=first_sem.at[j, a, h], recv_sem=slot_sem.at[i, h],
            device_id=(z * ratio + j, z), device_id_type=MESH,
        )

    def own_copy(j, a, h):
        i = (STEPS - 1) * actions + a
        return pltpu.make_async_copy(held(j, a, h), slots.at[i, h], own_sem.at[a, h])

    def for_blocks(away, own):
        for j in range(ratio):
            d = (z * ratio + j - b + rows) % rows

            @pl.when((d > 0) & (d < STEPS))
            def _():
                @pl.loop(0, actions)
                def _(a):
                    for h in range(PIECES):
                        away(j, d, a, h)

            if own is not None:
                @pl.when(d == 0)
                def _():
                    @pl.loop(0, actions)
                    def _(a):
                        for h in range(PIECES):
                            own(j, a, h)

    for_blocks(
        lambda j, d, a, h: first_copy(j, d, a, h).start(),
        lambda j, a, h: own_copy(j, a, h).start(),
    )

    def along(i, h, by, sem):
        return pltpu.make_async_remote_copy(
            src_ref=slots.at[i, h], dst_ref=slots.at[i, h],
            send_sem=sem.at[i, h], recv_sem=slot_sem.at[i, h],
            device_id=(b, z + by), device_id_type=MESH,
        )

    goes_up = (z >= q) & (z < cols - 1)
    goes_down = (z <= q) & (z > 0)

    def sum_copy(i):
        d = i // actions + 1
        return pltpu.make_async_remote_copy(
            src_ref=work.at[i], dst_ref=arrived.at[i],
            send_sem=sum_send.at[i], recv_sem=sum_recv.at[i],
            device_id=((b - d + rows) % rows, z), device_id_type=MESH,
        )

    def finish(a):
        for d in range(STEPS - 1):
            sum_copy(d * actions + a).wait_recv()

        @pl.loop(0, out_ref.shape[0] // 16)
        def _(k):
            at = pl.ds(pl.multiple_of(k * 16, 16), 16)
            backup = e_buf[a, at, :].astype(jnp.float32) + work[sums + a, at, :]
            for d in range(STEPS - 1):
                backup = backup + arrived[d * actions + a, at, :]
            cost = c_buf[a, at, :].astype(jnp.float32) + DISCOUNT * backup

            @pl.when(a == 0)
            def _():
                out_ref[at, :] = cost

            @pl.when(a > 0)
            def _():
                out_ref[at, :] = jnp.minimum(out_ref[at, :], cost)

    @pl.loop(0, total)
    def _(i):
        for h in range(PIECES):
            local = (i >= sums) & (z == q)

            @pl.when(local)
            def _():
                own_copy(b % ratio, i % actions, h).wait()

            @pl.when(jnp.logical_not(local))
            def _():
                along(i, h, 0, up_sem).wait_recv()

            @pl.when(goes_up)
            def _():
                along(i, h, 1, up_sem).start()

            @pl.when(goes_down)
            def _():
                along(i, h, -1, down_sem).start()

            if h == 0:
                @pl.when(i == 0)
                def _():
                    for load in loads:
                        load.wait()

            tile = 512

            @pl.loop(0, work.shape[2] // tile)
            def _(n):
                at = pl.ds(pl.multiple_of(n * tile, tile), tile)
                product = jnp.dot(
                    slots[i, h], v_buf[h * half:(h + 1) * half, at],
                    preferred_element_type=jnp.float32,
                )
                if h == 0:
                    work[i, :, at] = product
                else:
                    work[i, :, at] += product

        @pl.when((i >= 1) & (i <= sums))
        def _():
            sum_copy(i - 1).start()

        @pl.when(i > sums)
        def _():
            finish(i - 1 - sums)

    finish(actions - 1)

    @pl.loop(0, sums)
    def _(i):
        sum_copy(i).wait_send()

    for_blocks(lambda j, d, a, h: first_copy(j, d, a, h).wait_send(), None)

    @pl.when(goes_up)
    def _():
        @pl.loop(0, total)
        def _(i):
            for h in range(PIECES):
                along(i, h, 1, up_sem).wait_send()

    @pl.when(goes_down)
    def _():
        @pl.loop(0, total)
        def _(i):
            for h in range(PIECES):
                along(i, h, -1, down_sem).wait_send()


def general(transitions, values, earlier_sum, section_costs):
    rows = lax.axis_size("row")
    cols = lax.axis_size("col")
    actions, height, _ = transitions.shape
    width, scenarios = values.shape
    total = STEPS * actions
    sums = (STEPS - 1) * actions
    ratio = rows // cols
    anywhere = pl.BlockSpec(memory_space=pl.ANY)
    dma = pltpu.SemaphoreType.DMA
    return pl.pallas_call(
        functools.partial(general_kernel, rows, cols),
        out_shape=jax.ShapeDtypeStruct((height, scenarios), jnp.float32),
        in_specs=[anywhere] * 4,
        out_specs=pl.BlockSpec(memory_space=pltpu.VMEM),
        scratch_shapes=[
            pltpu.VMEM((total, PIECES, height, width // PIECES), jnp.bfloat16),
            pltpu.VMEM((width, scenarios), jnp.bfloat16),
            pltpu.VMEM((total, height, scenarios), jnp.float32),
            pltpu.VMEM((sums, height, scenarios), jnp.float32),
            pltpu.VMEM((actions, height, scenarios), jnp.bfloat16),
            pltpu.VMEM((actions, height, scenarios), jnp.bfloat16),
            dma((3,)),
            dma((actions, PIECES)),
            dma((total, PIECES)),
            dma((ratio, actions, PIECES)),
            dma((total, PIECES)),
            dma((total, PIECES)),
            dma((sums,)),
            dma((sums,)),
        ],
        compiler_params=pltpu.CompilerParams(
            collective_id=0, has_side_effects=True, vmem_limit_bytes=66_000_000
        ),
    )(transitions, values, earlier_sum, section_costs)


CHUNK = 256
LENT = 4
ACROSS = (
    ((2, 0), (1, 1)), ((2, 0), (0, 1)), ((3, 0), (2, 1)), ((3, 0), (1, 1)), ((3, 0), (0, 1)),
    ((5, 3), (4, 2)), ((4, 3), (6, 2)), ((5, 3), (7, 2)),
    ((0, 3), (5, 2)), ((1, 3), (4, 2)), ((2, 3), (7, 2)), ((3, 3), (6, 2)),
    ((4, 0), (1, 1)), ((5, 0), (0, 1)), ((6, 0), (3, 1)), ((7, 0), (2, 1)),
)


def routed_kernel(
    t_ref, v_ref, e_ref, c_ref, out_ref, relay,
    slots, v_buf, acc, arr, e_buf, c_buf,
    in_sem, slot_sem, relay_sem, first_sem, direct_sem, alt_sem, fwd_sem, minor_sem, disp_sem,
    relay_z_sem, relay_in_sem, relay_x_sem, sum_send, sum_recv, there_sem,
):
    b = lax.axis_index("row")
    z = lax.axis_index("col")
    rows = 8
    k = b // 2
    odd = b % 2
    actions, height, _ = t_ref.shape
    width, scenarios = v_ref.shape
    pieces = width // CHUNK
    half = pieces // 2

    loads = [
        pltpu.make_async_copy(v_ref, v_buf, in_sem.at[0]),
        pltpu.make_async_copy(e_ref, e_buf, in_sem.at[1]),
        pltpu.make_async_copy(c_ref, c_buf, in_sem.at[2]),
    ]
    for load in loads:
        load.start()

    barrier = pltpu.get_barrier_semaphore()
    for by in range(1, rows):
        pl.semaphore_signal(barrier, inc=1, device_id=((b + by) % rows, z), device_id_type=MESH)

    @pl.when(z > 0)
    def _():
        pl.semaphore_signal(barrier, inc=1, device_id=(b, z - 1), device_id_type=MESH)

    @pl.when(z < 3)
    def _():
        pl.semaphore_signal(barrier, inc=1, device_id=(b, z + 1), device_id_type=MESH)

    greeted = rows - 1 + jnp.where(z > 0, 1, 0) + jnp.where(z < 3, 1, 0)
    for (to, by) in ACROSS:
        @pl.when((b == to[0]) & (z == to[1]))
        def _():
            pl.semaphore_signal(barrier, inc=1, device_id=by, device_id_type=MESH)

        greeted = greeted + jnp.where((b == by[0]) & (z == by[1]), 1, 0)
    pl.semaphore_wait(barrier, greeted)

    def remote(src, dst, send, recv, to):
        return pltpu.make_async_remote_copy(
            src_ref=src, dst_ref=dst, send_sem=send, recv_sem=recv, device_id=to, device_id_type=MESH
        )

    side = jnp.where(z < 2, 1, -1)

    def held(j, h):
        return t_ref.at[:, :, pl.ds(pl.multiple_of(j * width + h * CHUNK, 128), CHUNK)]

    def own_copy(j, h):
        return pltpu.make_async_copy(held(j, h), slots.at[0, h], slot_sem.at[0, h])

    def first_copy(j, d, h):
        return remote(held(j, h), slots.at[d, h], first_sem.at[j, h], slot_sem.at[d, h], (2 * z + j, z))

    def direct_copy(j, d, h):
        to = jnp.where(z == 1, 0, 3)
        return remote(held(j, h), slots.at[d, h], direct_sem.at[j, h], slot_sem.at[d, h], (2 * z + j, to))

    def far_copy(h):
        return remote(held(0, h), relay.at[0, h], alt_sem.at[0, h], relay_sem.at[0, h], (b, z + side))

    def aside_copy(h):
        return remote(held(1, h), relay.at[0, h], alt_sem.at[1, h], relay_sem.at[0, h], ((b + 3) % rows, z))

    dist = [(2 * z + j - b + rows) % rows for j in range(2)]
    is_far = dist[0] == 3
    is_aside = dist[1] == 0

    def sends_cross(j):
        return (z == 1) & (dist[j] > j) & (dist[j] <= 2 + j)

    def sends_near(j):
        return ((z == 1) | (z == 2)) & (dist[j] <= j)

    far_later = is_far & (z % 2 == 0)
    later = (z == 2) & (dist[0] == 1)

    def every(condition, do):
        @pl.when(condition)
        def _():
            @pl.loop(0, pieces)
            def _(h):
                do(h)

    def first_both(h):
        for j in range(2):
            first_copy(j, dist[j], h).start()

    firsts = [(dist[j] > 0) & (dist[j] <= 2 + j) & jnp.logical_not(later) for j in range(2)]
    every(firsts[0] & firsts[1], first_both)
    every(firsts[0] & jnp.logical_not(firsts[1]), lambda h: first_copy(0, dist[0], h).start())
    every(firsts[1] & jnp.logical_not(firsts[0]), lambda h: first_copy(1, dist[1], h).start())
    every(is_far, lambda h: far_copy(h).start())
    every(is_far & jnp.logical_not(far_later), lambda h: first_copy(0, 3, h).start())
    for j in range(2):
        every(dist[j] == 0, lambda h: own_copy(j, h).start())
    every(is_aside, lambda h: aside_copy(h).start())

    @pl.loop(0, STEPS)
    def _(d):
        @pl.loop(0, actions)
        def _(a):
            acc[d, a] = jnp.zeros(acc.shape[2:], jnp.float32)

    way = jnp.where(k < 2, 1, -1)
    chained = (k < 2) & (z >= k) & (z < 3) | (k >= 2) & (z <= k) & (z > 0)
    turns = (odd == 0) & (z == k) & ((k == 1) | (k == 2))
    crosses = (z == 2) & (k == 2)

    def chain_copy(d, h):
        return remote(slots.at[d, h], slots.at[d, h], fwd_sem.at[d, h], slot_sem.at[d, h], (b, z + way))

    lends = (b == 3) & (z == 2)

    def in_chain(d, h):
        return chained & (d < 3 + odd) & (d >= odd) | lends & (d == 0) & (h < LENT)

    def turn_copy(h):
        return remote(slots.at[3, h], slots.at[3, h], minor_sem.at[h], slot_sem.at[3, h], (b, z - way))

    def cross_copy(x, h):
        return remote(
            slots.at[1 + odd + x, h], relay.at[1 + x, h], disp_sem.at[x, h], relay_sem.at[1 + x, h], (b + 2, z)
        )

    def is_cross(d):
        return crosses & (d > odd) & (d <= 2 + odd)

    kr = (b // 2 + 2) % 4
    br = jnp.where(odd == 1, (b + 3) % rows, (b + 5) % rows)
    dr = jnp.where(odd == 1, 3, 0)
    way_r = jnp.where(kr < 2, 1, -1)
    relays = (kr < 2) & (z >= kr) | (kr >= 2) & (z <= kr)
    takes = relays & ((z != kr) | (odd == 0)) & (z + way_r >= 0) & (z + way_r <= 3)
    ends = takes & ((z + way_r == 0) | (z + way_r == 3))
    passes = takes & jnp.logical_not(ends)
    borrows = (b == 6) & (z == 2)
    splits = (b == 4) & (z == 2)
    hands = takes & (z != kr)
    lifts = (z == 2) & (k == 3)

    def pass_copy(h):
        return remote(relay.at[0, h], relay.at[0, h], relay_z_sem.at[h], relay_sem.at[0, h], (b, z + way_r))

    def end_copy(h):
        return remote(
            relay.at[0, h], slots.at[dr, h], relay_z_sem.at[h], slot_sem.at[dr, h], (br, z + way_r)
        )

    def hand_copy(h):
        return remote(relay.at[0, h], slots.at[dr, h], relay_in_sem.at[h], slot_sem.at[dr, h], (br, z))

    def lift_copy(x, h):
        d = 1 + odd + x
        return remote(relay.at[1 + x, h], slots.at[d, h], relay_x_sem.at[x, h], slot_sem.at[d, h], ((b + 6) % rows, 3))

    def relay_step(h):
        pltpu.make_async_copy(relay.at[0, h], relay.at[0, h], relay_sem.at[0, h]).wait()

        @pl.when(passes)
        def _():
            pass_copy(h).start()

        @pl.when(hands)
        def _():
            hand_copy(h).start()

    def process(d, h):
        pltpu.make_async_copy(slots.at[d, h], slots.at[d, h], slot_sem.at[d, h]).wait()

        @pl.when(in_chain(d, h))
        def _():
            chain_copy(d, h).start()

        @pl.when(turns & (d == 3))
        def _():
            turn_copy(h).start()

        @pl.when(is_cross(d))
        def _():
            cross_copy(d - 1 - odd, h).start()

        tile = 512

        @pl.loop(0, scenarios // tile)
        def _(n):
            at = pl.ds(pl.multiple_of(n * tile, tile), tile)
            rows_at = pl.ds(pl.multiple_of(h * CHUNK, CHUNK), CHUNK)
            product = jnp.dot(
                slots[d, h].reshape(actions * height, CHUNK), v_buf[rows_at, at],
                preferred_element_type=jnp.float32,
            )
            acc[d, :, :, at] += product.reshape(actions, height, tile)

    def sum_copy(d, a):
        slot = jnp.where(odd == 1, jnp.where(d == 1, 2, 3 - d), jnp.where(d == 1, 2, 3))
        to = jnp.where(odd == 1, b - 1, (b - d + rows) % rows)
        return remote(acc.at[d, a], arr.at[slot, a], sum_send.at[d, a], sum_recv.at[slot, a], (to, z))

    def arrived(slot, a):
        pltpu.make_async_copy(arr.at[slot, a], arr.at[slot, a], sum_recv.at[slot, a]).wait()

    def send_sum(d):
        @pl.loop(0, actions)
        def _(a):
            sum_copy(d, a).start()

    def add_and_send(d):
        @pl.loop(0, actions)
        def _(a):
            arrived(2 - d, a)
            acc[d, a] += arr[2 - d, a]
            sum_copy(d, a).start()

    for load in loads:
        load.wait()

    near_each = jnp.where(k % 2 == 0, 4, 8)
    slow_end = (odd == 1) & ((z == 3) & (k < 2) | (z == 0) & (k == 2))
    own_from = jnp.where(slow_end, 24, pieces)
    in_turn = (k == 2) | (k == 1) & (z == 0)
    hops = jnp.where(z > k, z - k, k - z)
    far_from = jnp.where(hops == 0, jnp.where(k % 2 == 0, 16, 0), jnp.where(hops == 3, 6, 1 + 2 * hops))
    far_from = jnp.where((z == 0) & (b == 4) | (z == 3) & (b == 2), 7, jnp.where((z == 3) & (b == 4), 16, far_from))
    far_each = jnp.where(far_from >= 14, 4, 2)
    far_end = far_from + pieces // far_each
    hops_r = jnp.where(z > kr, z - kr, kr - z)
    relay_from = jnp.where(odd == 1, 2 * hops_r - 2, 2 * hops_r)
    end_from = jnp.where(odd == 1, jnp.where((kr == 0) | (kr == 3), 6, 4), jnp.where((kr == 0) | (kr == 3), 8, jnp.where(kr == 1, 18, 17)))

    @pl.loop(0, 2 * pieces)
    def _(g):
        for j in range(2):
            @pl.when(sends_cross(j) & (g < half) & (dist[j] == 2 + j))
            def _():
                for i in range(2):
                    direct_copy(j, dist[j], 2 * g + i).start()

            near_turn = jnp.where(z == 1, g >= 4, (g < half) | (g < pieces) & (g % 2 == 0) | (g >= 20))
            near_h = jnp.where(z == 1, g - 4, jnp.where(g < half, g, jnp.where(g < pieces, half + (g - half) // 2, g - 8)))

            @pl.when(sends_near(j) & near_turn & (near_h < pieces))
            def _():
                direct_copy(j, dist[j], near_h).start()

        @pl.when((z == 1) & (dist[0] == 1) & (g == half))
        def _():
            @pl.loop(0, pieces)
            def _(h):
                for j in range(2):
                    direct_copy(j, 1 + j, h).start()

        @pl.when(later & (g == 6))
        def _():
            @pl.loop(0, pieces)
            def _(h):
                for j in range(2):
                    first_copy(j, 1 + j, h).start()

        @pl.when(lifts & (g < pieces + 1) & (g != half))
        def _():
            for i in range(2):
                x, h = jnp.where(g < half, 1, 0), 2 * jnp.where(g < half, g, g - half - 1) + i
                pltpu.make_async_copy(relay.at[1 + x, h], relay.at[1 + x, h], relay_sem.at[1 + x, h]).wait()
                lift_copy(x, h).start()

        @pl.when(far_later & (g == 7))
        def _():
            @pl.loop(0, pieces)
            def _(h):
                first_copy(0, 3, h).start()

        @pl.loop(0, 7)
        def _(i):
            cross = g < pieces
            far_due = (g >= far_from) & (g < far_end) & (odd == 0) & (i < 3 + far_each)
            far_due = far_due | (odd == 1) & (g >= own_from) & (i == 3)
            d = jnp.where(i >= 3, 3 * (1 - odd), jnp.where(i == 2, odd, 2 + odd - jnp.where(in_turn, g // half, i)))
            h = jnp.where(i >= 3, jnp.where(odd == 1, g - own_from, far_each * (g - far_from) + i - 3), jnp.where(in_turn, 2 * (g % half) + i, g))
            h = jnp.where(i == 2, jnp.where(cross, g // near_each, g - pieces + pieces // near_each), h)
            near = jnp.where(cross, g % near_each == near_each - 1, g < 2 * pieces - pieces // near_each)

            @pl.when(jnp.where(i < 2, cross, jnp.where(i == 2, near, far_due)))
            def _():
                process(d, h)

        @pl.when(takes & (g >= relay_from) & (g < relay_from + half))
        def _():
            for i in range(2):
                relay_step(2 * (g - relay_from) + i)

        end_step = jnp.where(splits & (g >= 22), g - 20, jnp.where(splits & (g >= end_from + 2), 4, g - end_from))

        @pl.when(ends & (end_step >= 0) & (end_step < 4))
        def _():
            @pl.loop(0, pieces // 4)
            def _(i):
                h = pieces // 4 * end_step + i

                @pl.when(jnp.logical_not(borrows) | (h >= LENT))
                def _():
                    end_copy(h).start()

        first_at = jnp.where(in_turn & (z != 2), half, pieces)

        @pl.when((odd == 1) & (g == first_at - 1))
        def _():
            send_sum(3)

        @pl.when((odd == 1) & (g == pieces - 1))
        def _():
            send_sum(2)

        @pl.when((odd == 1) & (g == 2 * pieces - pieces // near_each - 1))
        def _():
            send_sum(1)

        @pl.when((z == 3) & (k == 2) & (g == pieces - 1))
        def _():
            pl.semaphore_signal(there_sem, inc=1, device_id=(6, 3), device_id_type=MESH)

        @pl.when((z == 3) & (b == 6) & (g == pieces + 1))
        def _():
            pl.semaphore_wait(there_sem, 2)

        @pl.when((odd == 0) & (g == first_at + 1))
        def _():
            add_and_send(2)

        @pl.when((odd == 0) & (g == pieces + jnp.where((z == 3) & (b == 4), 4, 2)))
        def _():
            add_and_send(1)

        @pl.when((odd == 0) & (g == jnp.where((b == 0) & (z == 2) | (b == 4) & (z == 0), 20, far_end - 1)))
        def _():
            send_sum(3)

    @pl.when(slow_end)
    def _():
        @pl.loop(half, pieces)
        def _(h):
            process(0, h)

    @pl.loop(0, actions)
    def _(a):
        arrived(2, a)
        arrived(3, a)

        @pl.loop(0, height // 16)
        def _(n):
            at = pl.ds(pl.multiple_of(n * 16, 16), 16)
            backup = e_buf[a, at, :].astype(jnp.float32) + acc[0, a, at, :] + arr[2, a, at, :] + arr[3, a, at, :]
            cost = c_buf[a, at, :].astype(jnp.float32) + DISCOUNT * backup

            @pl.when(a == 0)
            def _():
                out_ref[at, :] = cost

            @pl.when(a > 0)
            def _():
                out_ref[at, :] = jnp.minimum(out_ref[at, :], cost)

    @pl.loop(1, STEPS)
    def _(d):
        @pl.loop(0, actions)
        def _(a):
            sum_copy(d, a).wait_send()

    for j in range(2):
        every((dist[j] > 0) & (dist[j] < STEPS), lambda h: first_copy(j, dist[j], h).wait_send())
        every(sends_cross(j) | sends_near(j), lambda h: direct_copy(j, dist[j], h).wait_send())
    every(is_far, lambda h: far_copy(h).wait_send())
    every(is_aside, lambda h: aside_copy(h).wait_send())
    for d in range(1, STEPS):
        every(in_chain(d, pieces), lambda h: chain_copy(d, h).wait_send())

    @pl.loop(0, pieces)
    def _(h):
        @pl.when(in_chain(0, h))
        def _():
            chain_copy(0, h).wait_send()

        @pl.when(ends & (jnp.logical_not(borrows) | (h >= LENT)))
        def _():
            end_copy(h).wait_send()

    every(turns, lambda h: turn_copy(h).wait_send())
    every(passes, lambda h: pass_copy(h).wait_send())
    every(hands, lambda h: hand_copy(h).wait_send())
    for x in range(2):
        every(crosses, lambda h: cross_copy(x, h).wait_send())
        every(lifts, lambda h: lift_copy(x, h).wait_send())


def routed(transitions, values, earlier_sum, section_costs):
    actions, height, _ = transitions.shape
    width, scenarios = values.shape
    pieces = width // CHUNK
    anywhere = pl.BlockSpec(memory_space=pl.ANY)
    dma = pltpu.SemaphoreType.DMA
    return pl.pallas_call(
        routed_kernel,
        out_shape=(
            jax.ShapeDtypeStruct((height, scenarios), jnp.float32),
            jax.ShapeDtypeStruct((3, pieces, actions, height, CHUNK), jnp.bfloat16),
        ),
        in_specs=[anywhere] * 4,
        out_specs=(pl.BlockSpec(memory_space=pltpu.VMEM), anywhere),
        scratch_shapes=[
            pltpu.VMEM((STEPS, pieces, actions, height, CHUNK), jnp.bfloat16),
            pltpu.VMEM((width, scenarios), jnp.bfloat16),
            pltpu.VMEM((STEPS, actions, height, scenarios), jnp.float32),
            pltpu.VMEM((STEPS, actions, height, scenarios), jnp.float32),
            pltpu.VMEM((actions, height, scenarios), jnp.bfloat16),
            pltpu.VMEM((actions, height, scenarios), jnp.bfloat16),
            dma((3,)),
            dma((STEPS, pieces)),
            dma((3, pieces)),
            dma((2, pieces)),
            dma((2, pieces)),
            dma((2, pieces)),
            dma((STEPS, pieces)),
            dma((pieces,)),
            dma((2, pieces)),
            dma((pieces,)),
            dma((pieces,)),
            dma((2, pieces)),
            dma((STEPS, actions)),
            dma((STEPS, actions)),
            pltpu.SemaphoreType.REGULAR,
        ],
        compiler_params=pltpu.CompilerParams(
            collective_id=0, has_side_effects=True, vmem_limit_bytes=66_000_000
        ),
    )(transitions, values, earlier_sum, section_costs)[0]


def local(transitions, values, earlier_sum, section_costs):
    if lax.axis_size("row") == 8 and lax.axis_size("col") == 4:
        return routed(transitions, values, earlier_sum, section_costs)
    return general(transitions, values, earlier_sum, section_costs)


def solution(mesh):
    in_specs = (
        P(None, "row", "col"),
        P("row", "col"),
        P(None, "row", "col"),
        P(None, "row", "col"),
    )
    out_specs = P("row", "col")
    return jax.shard_map(local, mesh=mesh, in_specs=in_specs, out_specs=out_specs, check_vma=False)
```

```python
import functools

import jax
import jax.numpy as jnp
from jax import lax
from jax.experimental import pallas as pl
from jax.experimental.pallas import tpu as pltpu
from jax.sharding import PartitionSpec as P

STEPS = 4
PIECES = 8
DISCOUNT = 0.97
MESH = pl.DeviceIdType.MESH


def general_kernel(
    rows, cols, t_ref, v_ref, e_ref, c_ref, out_ref,
    slots, v_buf, work, arrived, e_buf, c_buf,
    in_sem, own_sem, slot_sem, first_sem, up_sem, down_sem, sum_send, sum_recv,
):
    b = lax.axis_index("row")
    z = lax.axis_index("col")
    ratio = rows // cols
    q = b // ratio
    actions = t_ref.shape[0]
    width = v_ref.shape[0]
    half = width // PIECES
    sums = (STEPS - 1) * actions
    total = STEPS * actions

    loads = [
        pltpu.make_async_copy(v_ref, v_buf, in_sem.at[0]),
        pltpu.make_async_copy(e_ref, e_buf, in_sem.at[1]),
        pltpu.make_async_copy(c_ref, c_buf, in_sem.at[2]),
    ]
    for load in loads:
        load.start()

    barrier = pltpu.get_barrier_semaphore()
    for d in range(1, STEPS):
        for by in (d, rows - d):
            pl.semaphore_signal(barrier, inc=1, device_id=((b + by) % rows, z), device_id_type=MESH)

    @pl.when(z > 0)
    def _():
        pl.semaphore_signal(barrier, inc=1, device_id=(b, z - 1), device_id_type=MESH)

    @pl.when(z < cols - 1)
    def _():
        pl.semaphore_signal(barrier, inc=1, device_id=(b, z + 1), device_id_type=MESH)

    beside = jnp.where(z > 0, 1, 0) + jnp.where(z < cols - 1, 1, 0)
    pl.semaphore_wait(barrier, 2 * (STEPS - 1) + beside)

    def held(j, a, h):
        offset = pl.multiple_of(j * width + h * half, 128)
        return t_ref.at[a, :, pl.ds(offset, half)]

    def first_copy(j, d, a, h):
        i = (d - 1) * actions + a
        return pltpu.make_async_remote_copy(
            src_ref=held(j, a, h), dst_ref=slots.at[i, h],
            send_sem=first_sem.at[j, a, h], recv_sem=slot_sem.at[i, h],
            device_id=(z * ratio + j, z), device_id_type=MESH,
        )

    def own_copy(j, a, h):
        i = (STEPS - 1) * actions + a
        return pltpu.make_async_copy(held(j, a, h), slots.at[i, h], own_sem.at[a, h])

    def for_blocks(away, own):
        for j in range(ratio):
            d = (z * ratio + j - b + rows) % rows

            @pl.when((d > 0) & (d < STEPS))
            def _():
                @pl.loop(0, actions)
                def _(a):
                    for h in range(PIECES):
                        away(j, d, a, h)

            if own is not None:
                @pl.when(d == 0)
                def _():
                    @pl.loop(0, actions)
                    def _(a):
                        for h in range(PIECES):
                            own(j, a, h)

    for_blocks(
        lambda j, d, a, h: first_copy(j, d, a, h).start(),
        lambda j, a, h: own_copy(j, a, h).start(),
    )

    def along(i, h, by, sem):
        return pltpu.make_async_remote_copy(
            src_ref=slots.at[i, h], dst_ref=slots.at[i, h],
            send_sem=sem.at[i, h], recv_sem=slot_sem.at[i, h],
            device_id=(b, z + by), device_id_type=MESH,
        )

    goes_up = (z >= q) & (z < cols - 1)
    goes_down = (z <= q) & (z > 0)

    def sum_copy(i):
        d = i // actions + 1
        return pltpu.make_async_remote_copy(
            src_ref=work.at[i], dst_ref=arrived.at[i],
            send_sem=sum_send.at[i], recv_sem=sum_recv.at[i],
            device_id=((b - d + rows) % rows, z), device_id_type=MESH,
        )

    def finish(a):
        for d in range(STEPS - 1):
            sum_copy(d * actions + a).wait_recv()

        @pl.loop(0, out_ref.shape[0] // 16)
        def _(k):
            at = pl.ds(pl.multiple_of(k * 16, 16), 16)
            backup = e_buf[a, at, :].astype(jnp.float32) + work[sums + a, at, :]
            for d in range(STEPS - 1):
                backup = backup + arrived[d * actions + a, at, :]
            cost = c_buf[a, at, :].astype(jnp.float32) + DISCOUNT * backup

            @pl.when(a == 0)
            def _():
                out_ref[at, :] = cost

            @pl.when(a > 0)
            def _():
                out_ref[at, :] = jnp.minimum(out_ref[at, :], cost)

    @pl.loop(0, total)
    def _(i):
        for h in range(PIECES):
            local = (i >= sums) & (z == q)

            @pl.when(local)
            def _():
                own_copy(b % ratio, i % actions, h).wait()

            @pl.when(jnp.logical_not(local))
            def _():
                along(i, h, 0, up_sem).wait_recv()

            @pl.when(goes_up)
            def _():
                along(i, h, 1, up_sem).start()

            @pl.when(goes_down)
            def _():
                along(i, h, -1, down_sem).start()

            if h == 0:
                @pl.when(i == 0)
                def _():
                    for load in loads:
                        load.wait()

            tile = 512

            @pl.loop(0, work.shape[2] // tile)
            def _(n):
                at = pl.ds(pl.multiple_of(n * tile, tile), tile)
                product = jnp.dot(
                    slots[i, h], v_buf[h * half:(h + 1) * half, at],
                    preferred_element_type=jnp.float32,
                )
                if h == 0:
                    work[i, :, at] = product
                else:
                    work[i, :, at] += product

        @pl.when((i >= 1) & (i <= sums))
        def _():
            sum_copy(i - 1).start()

        @pl.when(i > sums)
        def _():
            finish(i - 1 - sums)

    finish(actions - 1)

    @pl.loop(0, sums)
    def _(i):
        sum_copy(i).wait_send()

    for_blocks(lambda j, d, a, h: first_copy(j, d, a, h).wait_send(), None)

    @pl.when(goes_up)
    def _():
        @pl.loop(0, total)
        def _(i):
            for h in range(PIECES):
                along(i, h, 1, up_sem).wait_send()

    @pl.when(goes_down)
    def _():
        @pl.loop(0, total)
        def _(i):
            for h in range(PIECES):
                along(i, h, -1, down_sem).wait_send()


def general(transitions, values, earlier_sum, section_costs):
    rows = lax.axis_size("row")
    cols = lax.axis_size("col")
    actions, height, _ = transitions.shape
    width, scenarios = values.shape
    total = STEPS * actions
    sums = (STEPS - 1) * actions
    ratio = rows // cols
    anywhere = pl.BlockSpec(memory_space=pl.ANY)
    dma = pltpu.SemaphoreType.DMA
    return pl.pallas_call(
        functools.partial(general_kernel, rows, cols),
        out_shape=jax.ShapeDtypeStruct((height, scenarios), jnp.float32),
        in_specs=[anywhere] * 4,
        out_specs=pl.BlockSpec(memory_space=pltpu.VMEM),
        scratch_shapes=[
            pltpu.VMEM((total, PIECES, height, width // PIECES), jnp.bfloat16),
            pltpu.VMEM((width, scenarios), jnp.bfloat16),
            pltpu.VMEM((total, height, scenarios), jnp.float32),
            pltpu.VMEM((sums, height, scenarios), jnp.float32),
            pltpu.VMEM((actions, height, scenarios), jnp.bfloat16),
            pltpu.VMEM((actions, height, scenarios), jnp.bfloat16),
            dma((3,)),
            dma((actions, PIECES)),
            dma((total, PIECES)),
            dma((ratio, actions, PIECES)),
            dma((total, PIECES)),
            dma((total, PIECES)),
            dma((sums,)),
            dma((sums,)),
        ],
        compiler_params=pltpu.CompilerParams(
            collective_id=0, has_side_effects=True, vmem_limit_bytes=66_000_000
        ),
    )(transitions, values, earlier_sum, section_costs)


CHUNK = 256
LENT = 6
ACROSS = (
    ((2, 0), (1, 1)), ((2, 0), (0, 1)), ((3, 0), (2, 1)), ((3, 0), (1, 1)), ((3, 0), (0, 1)),
    ((5, 3), (4, 2)), ((4, 3), (6, 2)), ((5, 3), (7, 2)),
    ((0, 3), (5, 2)), ((1, 3), (4, 2)), ((2, 3), (7, 2)), ((3, 3), (6, 2)),
    ((4, 0), (1, 1)), ((5, 0), (0, 1)), ((6, 0), (3, 1)), ((7, 0), (2, 1)),
)


def routed_kernel(
    t_ref, v_ref, e_ref, c_ref, out_ref, relay,
    slots, v_buf, acc, arr, e_buf, c_buf,
    in_sem, value_sem, slot_sem, relay_sem, first_sem, direct_sem, alt_sem, fwd_sem, minor_sem, disp_sem,
    relay_z_sem, relay_in_sem, relay_x_sem, sum_send, sum_recv, there_sem,
):
    b = lax.axis_index("row")
    z = lax.axis_index("col")
    rows = 8
    k = b // 2
    odd = b % 2
    actions, height, _ = t_ref.shape
    width, scenarios = v_ref.shape
    pieces = width // CHUNK
    half = pieces // 2

    def every(condition, do):
        @pl.when(condition)
        def _():
            @pl.loop(0, pieces)
            def _(h):
                do(h)

    def held(j, h):
        return t_ref.at[:, :, pl.ds(pl.multiple_of(j * width + h * CHUNK, 128), CHUNK)]

    def own_copy(j, h):
        return pltpu.make_async_copy(held(j, h), slots.at[0, h], slot_sem.at[0, h])

    dist = [(2 * z + j - b + rows) % rows for j in range(2)]
    def value_copy(h):
        at = pl.ds(pl.multiple_of(h * CHUNK, CHUNK), CHUNK)
        return pltpu.make_async_copy(v_ref.at[at], v_buf.at[at], value_sem.at[h])

    @pl.loop(0, 4)
    def _(h):
        value_copy(h).start()

    for j in range(2):
        every(dist[j] == 0, lambda h: own_copy(j, h).start())

    @pl.loop(4, pieces)
    def _(h):
        value_copy(h).start()

    loads = [
        pltpu.make_async_copy(e_ref, e_buf, in_sem.at[0]),
        pltpu.make_async_copy(c_ref, c_buf, in_sem.at[1]),
    ]
    for load in loads:
        load.start()

    barrier = pltpu.get_barrier_semaphore()
    for by in range(1, rows):
        pl.semaphore_signal(barrier, inc=1, device_id=((b + by) % rows, z), device_id_type=MESH)

    @pl.when(z > 0)
    def _():
        pl.semaphore_signal(barrier, inc=1, device_id=(b, z - 1), device_id_type=MESH)

    @pl.when(z < 3)
    def _():
        pl.semaphore_signal(barrier, inc=1, device_id=(b, z + 1), device_id_type=MESH)

    greeted = rows - 1 + jnp.where(z > 0, 1, 0) + jnp.where(z < 3, 1, 0)
    for (to, by) in ACROSS:
        @pl.when((b == to[0]) & (z == to[1]))
        def _():
            pl.semaphore_signal(barrier, inc=1, device_id=by, device_id_type=MESH)

        greeted = greeted + jnp.where((b == by[0]) & (z == by[1]), 1, 0)
    pl.semaphore_wait(barrier, greeted)

    def remote(src, dst, send, recv, to):
        return pltpu.make_async_remote_copy(
            src_ref=src, dst_ref=dst, send_sem=send, recv_sem=recv, device_id=to, device_id_type=MESH
        )

    way = jnp.where(k < 2, 1, -1)
    chained = (k < 2) & (z >= k) & (z < 3) | (k >= 2) & (z <= k) & (z > 0)
    starts = chained & (z == k) & (odd == 0)
    before = jnp.where(k % 2 == 0, 4, 2)

    @pl.when(starts)
    def _():
        @pl.loop(0, before)
        def _(h):
            remote(held(0, h), slots.at[0, h], fwd_sem.at[0, h], slot_sem.at[0, h], (b, z + way)).start()

    side = jnp.where(z < 2, 1, -1)

    def first_copy(j, d, h):
        return remote(held(j, h), slots.at[d, h], first_sem.at[j, h], slot_sem.at[d, h], (2 * z + j, z))

    def direct_copy(j, d, h):
        to = jnp.where(z == 1, 0, 3)
        return remote(held(j, h), slots.at[d, h], direct_sem.at[j, h], slot_sem.at[d, h], (2 * z + j, to))

    def far_copy(h):
        return remote(held(0, h), relay.at[0, h], alt_sem.at[0, h], relay_sem.at[0, h], (b, z + side))

    def aside_copy(h):
        return remote(held(1, h), relay.at[0, h], alt_sem.at[1, h], relay_sem.at[0, h], ((b + 3) % rows, z))

    is_far = dist[0] == 3
    is_aside = dist[1] == 0

    def sends_cross(j):
        return (z == 1) & (dist[j] > j) & (dist[j] <= 2 + j)

    def sends_near(j):
        return ((z == 1) | (z == 2)) & (dist[j] <= j)

    far_later = is_far & (z % 2 == 0)
    later = (z == 2) & (dist[0] == 1)

    def first_both(h):
        for j in range(2):
            first_copy(j, dist[j], h).start()

    firsts = [(dist[j] > 0) & (dist[j] <= 2 + j) & jnp.logical_not(later) for j in range(2)]
    every(firsts[0] & firsts[1], first_both)
    every(firsts[0] & jnp.logical_not(firsts[1]), lambda h: first_copy(0, dist[0], h).start())
    every(firsts[1] & jnp.logical_not(firsts[0]), lambda h: first_copy(1, dist[1], h).start())
    every(is_far, lambda h: far_copy(h).start())
    every(is_far & jnp.logical_not(far_later), lambda h: first_copy(0, 3, h).start())
    every(is_aside, lambda h: aside_copy(h).start())

    turns = (odd == 0) & (z == k) & ((k == 1) | (k == 2))
    crosses = (z == 2) & (k == 2)

    def chain_copy(d, h):
        return remote(slots.at[d, h], slots.at[d, h], fwd_sem.at[d, h], slot_sem.at[d, h], (b, z + way))

    lends = (b == 3) & (z == 2)

    def in_chain(d, h):
        return chained & (d < 3 + odd) & (d >= odd) | lends & (d == 0) & (h < LENT)

    def turn_copy(h):
        return remote(slots.at[3, h], slots.at[3, h], minor_sem.at[h], slot_sem.at[3, h], (b, z - way))

    def cross_copy(x, h):
        return remote(
            slots.at[1 + odd + x, h], relay.at[1 + x, h], disp_sem.at[x, h], relay_sem.at[1 + x, h], (b + 2, z)
        )

    def is_cross(d):
        return crosses & (d > odd) & (d <= 2 + odd)

    kr = (b // 2 + 2) % 4
    br = jnp.where(odd == 1, (b + 3) % rows, (b + 5) % rows)
    dr = jnp.where(odd == 1, 3, 0)
    way_r = jnp.where(kr < 2, 1, -1)
    relays = (kr < 2) & (z >= kr) | (kr >= 2) & (z <= kr)
    takes = relays & ((z != kr) | (odd == 0)) & (z + way_r >= 0) & (z + way_r <= 3)
    ends = takes & ((z + way_r == 0) | (z + way_r == 3))
    passes = takes & jnp.logical_not(ends)
    borrows = (b == 6) & (z == 2)
    splits = (b == 4) & (z == 2)
    hands = takes & (z != kr)
    lifts = (z == 2) & (k == 3)

    def pass_copy(h):
        return remote(relay.at[0, h], relay.at[0, h], relay_z_sem.at[h], relay_sem.at[0, h], (b, z + way_r))

    def end_copy(h):
        return remote(
            relay.at[0, h], slots.at[dr, h], relay_z_sem.at[h], slot_sem.at[dr, h], (br, z + way_r)
        )

    def hand_copy(h):
        return remote(relay.at[0, h], slots.at[dr, h], relay_in_sem.at[h], slot_sem.at[dr, h], (br, z))

    def lift_copy(x, h):
        d = 1 + odd + x
        return remote(relay.at[1 + x, h], slots.at[d, h], relay_x_sem.at[x, h], slot_sem.at[d, h], ((b + 6) % rows, 3))

    def relay_step(h):
        pltpu.make_async_copy(relay.at[0, h], relay.at[0, h], relay_sem.at[0, h]).wait()

        @pl.when(passes)
        def _():
            pass_copy(h).start()

        @pl.when(hands)
        def _():
            hand_copy(h).start()

    def process(d, h):
        pltpu.make_async_copy(slots.at[d, h], slots.at[d, h], slot_sem.at[d, h]).wait()

        @pl.when(in_chain(d, h) & jnp.logical_not(starts & (d == 0) & (h < before)))
        def _():
            chain_copy(d, h).start()

        @pl.when(turns & (d == 3))
        def _():
            turn_copy(h).start()

        @pl.when(is_cross(d))
        def _():
            cross_copy(d - 1 - odd, h).start()

        tile = 512

        @pl.loop(0, scenarios // tile)
        def _(n):
            at = pl.ds(pl.multiple_of(n * tile, tile), tile)
            rows_at = pl.ds(pl.multiple_of(h * CHUNK, CHUNK), CHUNK)
            product = jnp.dot(
                slots[d, h].reshape(actions * height, CHUNK), v_buf[rows_at, at],
                preferred_element_type=jnp.float32,
            )
            product = product.reshape(actions, height, tile)
            acc[d, :, :, at] = jnp.where(h == 0, product, acc[d, :, :, at] + product)

    def sum_copy(d, a):
        slot = jnp.where(odd == 1, jnp.where(d == 1, 2, 3 - d), jnp.where(d == 1, 2, 3))
        to = jnp.where(odd == 1, b - 1, (b - d + rows) % rows)
        return remote(acc.at[d, a], arr.at[slot, a], sum_send.at[d, a], sum_recv.at[slot, a], (to, z))

    def arrived(slot, a):
        pltpu.make_async_copy(arr.at[slot, a], arr.at[slot, a], sum_recv.at[slot, a]).wait()

    def send_sum(d):
        @pl.loop(0, actions)
        def _(a):
            sum_copy(d, a).start()

    def add_and_send(d):
        @pl.loop(0, actions)
        def _(a):
            arrived(2 - d, a)
            acc[d, a] += arr[2 - d, a]
            sum_copy(d, a).start()

    @pl.loop(0, 4)
    def _(h):
        value_copy(h).wait()

    slow_end = (odd == 1) & ((z == 3) & (k < 2) | (z == 0) & (k == 2))
    own_from = jnp.where(slow_end, 24, jnp.where((b == 3) & (z == 0), half, pieces))
    in_turn = (k == 2) | (k == 1) & (z == 0)
    hops = jnp.where(z > k, z - k, k - z)
    far_from = jnp.where(hops == 0, jnp.where(k % 2 == 0, 16, 0), jnp.where(hops == 3, 6, 1 + 2 * hops))
    far_from = jnp.where((z == 0) & (b == 4) | (z == 3) & (b == 2), 7, jnp.where((z == 3) & (b == 4), 16, far_from))
    ahead = (b == 2) & (z == 0)
    far_each = jnp.where((far_from >= 14) | ahead, 4, 2)
    far_end = far_from + pieces // far_each
    hops_r = jnp.where(z > kr, z - kr, kr - z)
    relay_from = jnp.where(odd == 1, 2 * hops_r - 2, 2 * hops_r)
    end_from = jnp.where(odd == 1, jnp.where((kr == 0) | (kr == 3), 6, 4), jnp.where((kr == 0) | (kr == 3), 8, jnp.where(kr == 1, 18, 17)))

    @pl.loop(0, 2 * pieces)
    def _(g):
        @pl.when((g > 0) & (g < half - 1))
        def _():
            for i in range(2):
                value_copy(2 * g + 2 + i).wait()

        @pl.when(ahead & (g == half))
        def _():
            add_and_send(2)

        @pl.when((z == 1) & (dist[0] == 2) & (g < pieces // 4))
        def _():
            for i in range(4):
                for j in range(2):
                    direct_copy(j, 2 + j, 4 * g + i).start()

        for j in range(2):
            near_turn = jnp.where(z == 1, (g < 2) | (g >= 6), (g < half) | (g < pieces) & (g % 2 == 0) | (g >= 20))
            near_h = jnp.where(z == 1, jnp.where(g < 2, g, g - 4), jnp.where(g < half, g, jnp.where(g < pieces, half + (g - half) // 2, g - 8)))

            @pl.when(sends_near(j) & near_turn & (near_h < pieces))
            def _():
                direct_copy(j, dist[j], near_h).start()

        @pl.when((z == 1) & (dist[0] == 1) & (g == half + 1))
        def _():
            @pl.loop(0, pieces)
            def _(h):
                for j in range(2):
                    direct_copy(j, 1 + j, h).start()

        @pl.when(later & (g == 6))
        def _():
            @pl.loop(0, pieces)
            def _(h):
                for j in range(2):
                    first_copy(j, 1 + j, h).start()

        @pl.when(lifts & (g < pieces + 1) & (g != half))
        def _():
            for i in range(2):
                x, h = jnp.where(g < half, 1, 0), 2 * jnp.where(g < half, g, g - half - 1) + i
                pltpu.make_async_copy(relay.at[1 + x, h], relay.at[1 + x, h], relay_sem.at[1 + x, h]).wait()
                lift_copy(x, h).start()

        @pl.when(far_later & (g == 7))
        def _():
            @pl.loop(0, pieces)
            def _(h):
                first_copy(0, 3, h).start()

        @pl.loop(0, 8)
        def _(i):
            cross = g < pieces
            far_due = (g >= far_from) & (g < far_end) & (odd == 0) & (i < 4 + far_each)
            far_due = far_due | (odd == 1) & (g >= own_from) & (g < own_from + pieces) & (i == 4)
            middle = (k % 2 == 0) & ((g == 5) | (g == 10))
            near = (g == 0) | middle | (g >= pieces) & (g < 2 * pieces - before)
            d = jnp.where(i >= 4, 3 * (1 - odd), jnp.where(i < 2, odd, 2 + odd - jnp.where(in_turn, g // half, i - 2)))
            h = jnp.where(in_turn, 2 * (g % half) + i - 2, g)
            h = jnp.where(i >= 4, jnp.where(odd == 1, g - own_from, far_each * (g - far_from) + i - 4), h)
            h = jnp.where(i < 2, jnp.where(cross, jnp.where(g == 0, i, 1 + g // 5), g - pieces + before), h)

            @pl.when(jnp.where(i == 0, near, jnp.where(i == 1, g == 0, jnp.where(i < 4, cross, far_due))))
            def _():
                process(d, h)

        @pl.when(takes & (g >= relay_from) & (g < relay_from + half))
        def _():
            for i in range(2):
                relay_step(2 * (g - relay_from) + i)

        end_step = jnp.where(splits & (g >= 22), g - 20, jnp.where(splits & (g >= end_from + 2), 4, g - end_from))

        @pl.when(ends & (end_step >= 0) & (end_step < 4))
        def _():
            @pl.loop(0, pieces // 4)
            def _(i):
                h = pieces // 4 * end_step + i

                @pl.when(jnp.logical_not(borrows) | (h >= LENT))
                def _():
                    end_copy(h).start()

        first_at = jnp.where(in_turn & (z != 2), half, pieces)

        @pl.when((odd == 1) & (g == first_at - 1))
        def _():
            send_sum(3)

        @pl.when((odd == 1) & (g == pieces - 1))
        def _():
            send_sum(2)

        @pl.when((odd == 1) & (g == 2 * pieces - before - 1))
        def _():
            send_sum(1)

        @pl.when((z == 3) & (k == 2) & (g == pieces - 3))
        def _():
            pl.semaphore_signal(there_sem, inc=1, device_id=(6, 3), device_id_type=MESH)

        @pl.when((z == 3) & (b == 6) & (g == pieces + 1))
        def _():
            pl.semaphore_wait(there_sem, 2)

        @pl.when((odd == 0) & jnp.logical_not(ahead) & (g == first_at + 1))
        def _():
            add_and_send(2)

        @pl.when((odd == 0) & (g == pieces + jnp.where((z == 3) & (b == 4), 4, 2)))
        def _():
            add_and_send(1)

        @pl.when((odd == 0) & (g == jnp.where((b == 0) & (z == 2) | (b == 4) & (z == 0), 20, far_end - 1)))
        def _():
            send_sum(3)

    @pl.when(slow_end)
    def _():
        @pl.loop(half, pieces)
        def _(h):
            process(0, h)

    @pl.loop(1, STEPS)
    def _(d):
        @pl.loop(0, actions)
        def _(a):
            sum_copy(d, a).wait_send()

    for j in range(2):
        every((dist[j] > 0) & (dist[j] < STEPS), lambda h: first_copy(j, dist[j], h).wait_send())
        every(sends_cross(j) | sends_near(j), lambda h: direct_copy(j, dist[j], h).wait_send())
    every(is_far, lambda h: far_copy(h).wait_send())
    every(is_aside, lambda h: aside_copy(h).wait_send())
    for d in range(1, STEPS):
        every(in_chain(d, pieces), lambda h: chain_copy(d, h).wait_send())

    @pl.loop(0, pieces)
    def _(h):
        @pl.when(in_chain(0, h))
        def _():
            chain_copy(0, h).wait_send()

        @pl.when(ends & (jnp.logical_not(borrows) | (h >= LENT)))
        def _():
            end_copy(h).wait_send()

    every(turns, lambda h: turn_copy(h).wait_send())
    every(passes, lambda h: pass_copy(h).wait_send())
    every(hands, lambda h: hand_copy(h).wait_send())
    for x in range(2):
        every(crosses, lambda h: cross_copy(x, h).wait_send())
        every(lifts, lambda h: lift_copy(x, h).wait_send())

    for load in loads:
        load.wait()

    @pl.loop(0, actions)
    def _(a):
        arrived(2, a)
        arrived(3, a)

        @pl.loop(0, height // 16)
        def _(n):
            at = pl.ds(pl.multiple_of(n * 16, 16), 16)
            backup = e_buf[a, at, :].astype(jnp.float32) + acc[0, a, at, :] + arr[2, a, at, :] + arr[3, a, at, :]
            cost = c_buf[a, at, :].astype(jnp.float32) + DISCOUNT * backup

            @pl.when(a == 0)
            def _():
                out_ref[at, :] = cost

            @pl.when(a > 0)
            def _():
                out_ref[at, :] = jnp.minimum(out_ref[at, :], cost)


def routed(transitions, values, earlier_sum, section_costs):
    actions, height, _ = transitions.shape
    width, scenarios = values.shape
    pieces = width // CHUNK
    anywhere = pl.BlockSpec(memory_space=pl.ANY)
    dma = pltpu.SemaphoreType.DMA
    return pl.pallas_call(
        routed_kernel,
        out_shape=(
            jax.ShapeDtypeStruct((height, scenarios), jnp.float32),
            jax.ShapeDtypeStruct((3, pieces, actions, height, CHUNK), jnp.bfloat16),
        ),
        in_specs=[anywhere] * 4,
        out_specs=(pl.BlockSpec(memory_space=pltpu.VMEM), anywhere),
        scratch_shapes=[
            pltpu.VMEM((STEPS, pieces, actions, height, CHUNK), jnp.bfloat16),
            pltpu.VMEM((width, scenarios), jnp.bfloat16),
            pltpu.VMEM((STEPS, actions, height, scenarios), jnp.float32),
            pltpu.VMEM((STEPS, actions, height, scenarios), jnp.float32),
            pltpu.VMEM((actions, height, scenarios), jnp.bfloat16),
            pltpu.VMEM((actions, height, scenarios), jnp.bfloat16),
            dma((2,)),
            dma((pieces,)),
            dma((STEPS, pieces)),
            dma((3, pieces)),
            dma((2, pieces)),
            dma((2, pieces)),
            dma((2, pieces)),
            dma((STEPS, pieces)),
            dma((pieces,)),
            dma((2, pieces)),
            dma((pieces,)),
            dma((pieces,)),
            dma((2, pieces)),
            dma((STEPS, actions)),
            dma((STEPS, actions)),
            pltpu.SemaphoreType.REGULAR,
        ],
        compiler_params=pltpu.CompilerParams(
            collective_id=0, has_side_effects=True, vmem_limit_bytes=66_000_000
        ),
    )(transitions, values, earlier_sum, section_costs)[0]


def local(transitions, values, earlier_sum, section_costs):
    if lax.axis_size("row") == 8 and lax.axis_size("col") == 4:
        return routed(transitions, values, earlier_sum, section_costs)
    return general(transitions, values, earlier_sum, section_costs)


def solution(mesh):
    in_specs = (
        P(None, "row", "col"),
        P("row", "col"),
        P(None, "row", "col"),
        P(None, "row", "col"),
    )
    out_specs = P("row", "col")
    return jax.shard_map(local, mesh=mesh, in_specs=in_specs, out_specs=out_specs, check_vma=False)
```

```python
import functools

import jax
import jax.numpy as jnp
from jax import lax
from jax.experimental import pallas as pl
from jax.experimental.pallas import tpu as pltpu
from jax.sharding import PartitionSpec as P

STEPS = 4
PIECES = 8
DISCOUNT = 0.97
MESH = pl.DeviceIdType.MESH


def general_kernel(
    rows, cols, t_ref, v_ref, e_ref, c_ref, out_ref,
    slots, v_buf, work, arrived, e_buf, c_buf,
    in_sem, own_sem, slot_sem, first_sem, up_sem, down_sem, sum_send, sum_recv,
):
    b = lax.axis_index("row")
    z = lax.axis_index("col")
    ratio = rows // cols
    q = b // ratio
    actions = t_ref.shape[0]
    width = v_ref.shape[0]
    half = width // PIECES
    sums = (STEPS - 1) * actions
    total = STEPS * actions

    loads = [
        pltpu.make_async_copy(v_ref, v_buf, in_sem.at[0]),
        pltpu.make_async_copy(e_ref, e_buf, in_sem.at[1]),
        pltpu.make_async_copy(c_ref, c_buf, in_sem.at[2]),
    ]
    for load in loads:
        load.start()

    barrier = pltpu.get_barrier_semaphore()
    for d in range(1, STEPS):
        for by in (d, rows - d):
            pl.semaphore_signal(barrier, inc=1, device_id=((b + by) % rows, z), device_id_type=MESH)

    @pl.when(z > 0)
    def _():
        pl.semaphore_signal(barrier, inc=1, device_id=(b, z - 1), device_id_type=MESH)

    @pl.when(z < cols - 1)
    def _():
        pl.semaphore_signal(barrier, inc=1, device_id=(b, z + 1), device_id_type=MESH)

    beside = jnp.where(z > 0, 1, 0) + jnp.where(z < cols - 1, 1, 0)
    pl.semaphore_wait(barrier, 2 * (STEPS - 1) + beside)

    def held(j, a, h):
        offset = pl.multiple_of(j * width + h * half, 128)
        return t_ref.at[a, :, pl.ds(offset, half)]

    def first_copy(j, d, a, h):
        i = (d - 1) * actions + a
        return pltpu.make_async_remote_copy(
            src_ref=held(j, a, h), dst_ref=slots.at[i, h],
            send_sem=first_sem.at[j, a, h], recv_sem=slot_sem.at[i, h],
            device_id=(z * ratio + j, z), device_id_type=MESH,
        )

    def own_copy(j, a, h):
        i = (STEPS - 1) * actions + a
        return pltpu.make_async_copy(held(j, a, h), slots.at[i, h], own_sem.at[a, h])

    def for_blocks(away, own):
        for j in range(ratio):
            d = (z * ratio + j - b + rows) % rows

            @pl.when((d > 0) & (d < STEPS))
            def _():
                @pl.loop(0, actions)
                def _(a):
                    for h in range(PIECES):
                        away(j, d, a, h)

            if own is not None:
                @pl.when(d == 0)
                def _():
                    @pl.loop(0, actions)
                    def _(a):
                        for h in range(PIECES):
                            own(j, a, h)

    for_blocks(
        lambda j, d, a, h: first_copy(j, d, a, h).start(),
        lambda j, a, h: own_copy(j, a, h).start(),
    )

    def along(i, h, by, sem):
        return pltpu.make_async_remote_copy(
            src_ref=slots.at[i, h], dst_ref=slots.at[i, h],
            send_sem=sem.at[i, h], recv_sem=slot_sem.at[i, h],
            device_id=(b, z + by), device_id_type=MESH,
        )

    goes_up = (z >= q) & (z < cols - 1)
    goes_down = (z <= q) & (z > 0)

    def sum_copy(i):
        d = i // actions + 1
        return pltpu.make_async_remote_copy(
            src_ref=work.at[i], dst_ref=arrived.at[i],
            send_sem=sum_send.at[i], recv_sem=sum_recv.at[i],
            device_id=((b - d + rows) % rows, z), device_id_type=MESH,
        )

    def finish(a):
        for d in range(STEPS - 1):
            sum_copy(d * actions + a).wait_recv()

        @pl.loop(0, out_ref.shape[0] // 16)
        def _(k):
            at = pl.ds(pl.multiple_of(k * 16, 16), 16)
            backup = e_buf[a, at, :].astype(jnp.float32) + work[sums + a, at, :]
            for d in range(STEPS - 1):
                backup = backup + arrived[d * actions + a, at, :]
            cost = c_buf[a, at, :].astype(jnp.float32) + DISCOUNT * backup

            @pl.when(a == 0)
            def _():
                out_ref[at, :] = cost

            @pl.when(a > 0)
            def _():
                out_ref[at, :] = jnp.minimum(out_ref[at, :], cost)

    @pl.loop(0, total)
    def _(i):
        for h in range(PIECES):
            local = (i >= sums) & (z == q)

            @pl.when(local)
            def _():
                own_copy(b % ratio, i % actions, h).wait()

            @pl.when(jnp.logical_not(local))
            def _():
                along(i, h, 0, up_sem).wait_recv()

            @pl.when(goes_up)
            def _():
                along(i, h, 1, up_sem).start()

            @pl.when(goes_down)
            def _():
                along(i, h, -1, down_sem).start()

            if h == 0:
                @pl.when(i == 0)
                def _():
                    for load in loads:
                        load.wait()

            tile = 512

            @pl.loop(0, work.shape[2] // tile)
            def _(n):
                at = pl.ds(pl.multiple_of(n * tile, tile), tile)
                product = jnp.dot(
                    slots[i, h], v_buf[h * half:(h + 1) * half, at],
                    preferred_element_type=jnp.float32,
                )
                if h == 0:
                    work[i, :, at] = product
                else:
                    work[i, :, at] += product

        @pl.when((i >= 1) & (i <= sums))
        def _():
            sum_copy(i - 1).start()

        @pl.when(i > sums)
        def _():
            finish(i - 1 - sums)

    finish(actions - 1)

    @pl.loop(0, sums)
    def _(i):
        sum_copy(i).wait_send()

    for_blocks(lambda j, d, a, h: first_copy(j, d, a, h).wait_send(), None)

    @pl.when(goes_up)
    def _():
        @pl.loop(0, total)
        def _(i):
            for h in range(PIECES):
                along(i, h, 1, up_sem).wait_send()

    @pl.when(goes_down)
    def _():
        @pl.loop(0, total)
        def _(i):
            for h in range(PIECES):
                along(i, h, -1, down_sem).wait_send()


def general(transitions, values, earlier_sum, section_costs):
    rows = lax.axis_size("row")
    cols = lax.axis_size("col")
    actions, height, _ = transitions.shape
    width, scenarios = values.shape
    total = STEPS * actions
    sums = (STEPS - 1) * actions
    ratio = rows // cols
    anywhere = pl.BlockSpec(memory_space=pl.ANY)
    dma = pltpu.SemaphoreType.DMA
    return pl.pallas_call(
        functools.partial(general_kernel, rows, cols),
        out_shape=jax.ShapeDtypeStruct((height, scenarios), jnp.float32),
        in_specs=[anywhere] * 4,
        out_specs=pl.BlockSpec(memory_space=pltpu.VMEM),
        scratch_shapes=[
            pltpu.VMEM((total, PIECES, height, width // PIECES), jnp.bfloat16),
            pltpu.VMEM((width, scenarios), jnp.bfloat16),
            pltpu.VMEM((total, height, scenarios), jnp.float32),
            pltpu.VMEM((sums, height, scenarios), jnp.float32),
            pltpu.VMEM((actions, height, scenarios), jnp.bfloat16),
            pltpu.VMEM((actions, height, scenarios), jnp.bfloat16),
            dma((3,)),
            dma((actions, PIECES)),
            dma((total, PIECES)),
            dma((ratio, actions, PIECES)),
            dma((total, PIECES)),
            dma((total, PIECES)),
            dma((sums,)),
            dma((sums,)),
        ],
        compiler_params=pltpu.CompilerParams(
            collective_id=0, has_side_effects=True, vmem_limit_bytes=66_000_000
        ),
    )(transitions, values, earlier_sum, section_costs)


CHUNK = 256
LENT = (2, 6)
ACROSS = (
    ((2, 0), (1, 1)), ((2, 0), (0, 1)), ((3, 0), (2, 1)), ((3, 0), (1, 1)), ((3, 0), (0, 1)),
    ((5, 3), (4, 2)), ((4, 3), (6, 2)), ((5, 3), (7, 2)),
    ((0, 3), (5, 2)), ((1, 3), (4, 2)), ((2, 3), (7, 2)), ((3, 3), (6, 2)),
    ((4, 0), (1, 1)), ((5, 0), (0, 1)), ((6, 0), (3, 1)), ((7, 0), (2, 1)),
)


def routed_kernel(
    t_ref, v_ref, e_ref, c_ref, out_ref, relay,
    slots, v_buf, acc, arr, e_buf, c_buf,
    in_sem, value_sem, slot_sem, relay_sem, first_sem, direct_sem, alt_sem, fwd_sem, minor_sem, disp_sem,
    relay_z_sem, relay_in_sem, relay_x_sem, sum_send, sum_recv, there_sem,
):
    b = lax.axis_index("row")
    z = lax.axis_index("col")
    rows = 8
    k = b // 2
    odd = b % 2
    actions, height, _ = t_ref.shape
    width, scenarios = v_ref.shape
    pieces = width // CHUNK
    half = pieces // 2

    def every(condition, do):
        @pl.when(condition)
        def _():
            @pl.loop(0, pieces)
            def _(h):
                do(h)

    def held(j, h):
        return t_ref.at[:, :, pl.ds(pl.multiple_of(j * width + h * CHUNK, 128), CHUNK)]

    def own_copy(j, h):
        return pltpu.make_async_copy(held(j, h), slots.at[0, h], slot_sem.at[0, h])

    dist = [(2 * z + j - b + rows) % rows for j in range(2)]
    def value_copy(h):
        at = pl.ds(pl.multiple_of(h * CHUNK, CHUNK), CHUNK)
        return pltpu.make_async_copy(v_ref.at[at], v_buf.at[at], value_sem.at[h])

    @pl.loop(0, 4)
    def _(h):
        value_copy(h).start()

    for j in range(2):
        every(dist[j] == 0, lambda h: own_copy(j, h).start())

    @pl.loop(4, pieces)
    def _(h):
        value_copy(h).start()

    loads = [
        pltpu.make_async_copy(e_ref, e_buf, in_sem.at[0]),
        pltpu.make_async_copy(c_ref, c_buf, in_sem.at[1]),
    ]
    for load in loads:
        load.start()

    barrier = pltpu.get_barrier_semaphore()
    for by in range(1, rows):
        pl.semaphore_signal(barrier, inc=1, device_id=((b + by) % rows, z), device_id_type=MESH)

    @pl.when(z > 0)
    def _():
        pl.semaphore_signal(barrier, inc=1, device_id=(b, z - 1), device_id_type=MESH)

    @pl.when(z < 3)
    def _():
        pl.semaphore_signal(barrier, inc=1, device_id=(b, z + 1), device_id_type=MESH)

    greeted = rows - 1 + jnp.where(z > 0, 1, 0) + jnp.where(z < 3, 1, 0)
    for (to, by) in ACROSS:
        @pl.when((b == to[0]) & (z == to[1]))
        def _():
            pl.semaphore_signal(barrier, inc=1, device_id=by, device_id_type=MESH)

        greeted = greeted + jnp.where((b == by[0]) & (z == by[1]), 1, 0)
    pl.semaphore_wait(barrier, greeted)

    def remote(src, dst, send, recv, to):
        return pltpu.make_async_remote_copy(
            src_ref=src, dst_ref=dst, send_sem=send, recv_sem=recv, device_id=to, device_id_type=MESH
        )

    way = jnp.where(k < 2, 1, -1)
    chained = (k < 2) & (z >= k) & (z < 3) | (k >= 2) & (z <= k) & (z > 0)
    starts = chained & (z == k) & (odd == 0)
    before = jnp.where(k % 2 == 0, 4, 2)

    @pl.when(starts)
    def _():
        @pl.loop(0, before)
        def _(h):
            remote(held(0, h), slots.at[0, h], fwd_sem.at[0, h], slot_sem.at[0, h], (b, z + way)).start()

    side = jnp.where(z < 2, 1, -1)

    def first_copy(j, d, h):
        return remote(held(j, h), slots.at[d, h], first_sem.at[j, h], slot_sem.at[d, h], (2 * z + j, z))

    def direct_copy(j, d, h):
        to = jnp.where(z == 1, 0, 3)
        return remote(held(j, h), slots.at[d, h], direct_sem.at[j, h], slot_sem.at[d, h], (2 * z + j, to))

    def far_copy(h):
        return remote(held(0, h), relay.at[0, h], alt_sem.at[0, h], relay_sem.at[0, h], (b, z + side))

    def aside_copy(h):
        return remote(held(1, h), relay.at[0, h], alt_sem.at[1, h], relay_sem.at[0, h], ((b + 3) % rows, z))

    is_far = dist[0] == 3
    is_aside = dist[1] == 0

    def sends_cross(j):
        return (z == 1) & (dist[j] > j) & (dist[j] <= 2 + j)

    def sends_near(j):
        return ((z == 1) | (z == 2)) & (dist[j] <= j)

    far_later = is_far & (z % 2 == 0)
    later = (z == 2) & (dist[0] == 1)

    def first_both(h):
        for j in range(2):
            first_copy(j, dist[j], h).start()

    firsts = [(dist[j] > 0) & (dist[j] <= 2 + j) & jnp.logical_not(later) for j in range(2)]
    every(firsts[0] & firsts[1], first_both)
    every(firsts[0] & jnp.logical_not(firsts[1]), lambda h: first_copy(0, dist[0], h).start())
    every(firsts[1] & jnp.logical_not(firsts[0]), lambda h: first_copy(1, dist[1], h).start())
    every(is_far, lambda h: far_copy(h).start())
    every(is_far & jnp.logical_not(far_later), lambda h: first_copy(0, 3, h).start())
    every(is_aside, lambda h: aside_copy(h).start())

    turns = (odd == 0) & (z == k) & ((k == 1) | (k == 2))
    crosses = (z == 2) & (k == 2)

    def chain_copy(d, h):
        return remote(slots.at[d, h], slots.at[d, h], fwd_sem.at[d, h], slot_sem.at[d, h], (b, z + way))

    lends = ((b == 1) | (b == 3)) & (z == 2)
    lent = jnp.where(k == 0, LENT[0], LENT[1])

    def in_chain(d, h):
        return chained & (d < 3 + odd) & (d >= odd) | lends & (d == 0) & (h < lent)

    def turn_copy(h):
        return remote(slots.at[3, h], slots.at[3, h], minor_sem.at[h], slot_sem.at[3, h], (b, z - way))

    def cross_copy(x, h):
        return remote(
            slots.at[1 + odd + x, h], relay.at[1 + x, h], disp_sem.at[x, h], relay_sem.at[1 + x, h], (b + 2, z)
        )

    def is_cross(d):
        return crosses & (d > odd) & (d <= 2 + odd)

    kr = (b // 2 + 2) % 4
    br = jnp.where(odd == 1, (b + 3) % rows, (b + 5) % rows)
    dr = jnp.where(odd == 1, 3, 0)
    way_r = jnp.where(kr < 2, 1, -1)
    relays = (kr < 2) & (z >= kr) | (kr >= 2) & (z <= kr)
    takes = relays & ((z != kr) | (odd == 0)) & (z + way_r >= 0) & (z + way_r <= 3)
    ends = takes & ((z + way_r == 0) | (z + way_r == 3))
    passes = takes & jnp.logical_not(ends)
    borrows = ((b == 4) | (b == 6)) & (z == 2)
    borrowed = jnp.where(k == 2, LENT[0], LENT[1])
    splits = (b == 4) & (z == 2)
    hands = takes & (z != kr)
    lifts = (z == 2) & (k == 3)

    def pass_copy(h):
        return remote(relay.at[0, h], relay.at[0, h], relay_z_sem.at[h], relay_sem.at[0, h], (b, z + way_r))

    def end_copy(h):
        return remote(
            relay.at[0, h], slots.at[dr, h], relay_z_sem.at[h], slot_sem.at[dr, h], (br, z + way_r)
        )

    def hand_copy(h):
        return remote(relay.at[0, h], slots.at[dr, h], relay_in_sem.at[h], slot_sem.at[dr, h], (br, z))

    def lift_copy(x, h):
        d = 1 + odd + x
        return remote(relay.at[1 + x, h], slots.at[d, h], relay_x_sem.at[x, h], slot_sem.at[d, h], ((b + 6) % rows, 3))

    def relay_step(h):
        pltpu.make_async_copy(relay.at[0, h], relay.at[0, h], relay_sem.at[0, h]).wait()

        @pl.when(passes)
        def _():
            pass_copy(h).start()

        @pl.when(hands)
        def _():
            hand_copy(h).start()

    def process(d, h):
        pltpu.make_async_copy(slots.at[d, h], slots.at[d, h], slot_sem.at[d, h]).wait()

        @pl.when(in_chain(d, h) & jnp.logical_not(starts & (d == 0) & (h < before)))
        def _():
            chain_copy(d, h).start()

        @pl.when(turns & (d == 3))
        def _():
            turn_copy(h).start()

        @pl.when(is_cross(d))
        def _():
            cross_copy(d - 1 - odd, h).start()

        tile = 1536

        @pl.loop(0, scenarios // tile)
        def _(n):
            at = pl.ds(pl.multiple_of(n * tile, tile), tile)
            rows_at = pl.ds(pl.multiple_of(h * CHUNK, CHUNK), CHUNK)
            product = jnp.dot(
                slots[d, h].reshape(actions * height, CHUNK), v_buf[rows_at, at],
                preferred_element_type=jnp.float32,
            )
            product = product.reshape(actions, height, tile)
            acc[d, :, :, at] = jnp.where(h == 0, product, acc[d, :, :, at] + product)

    def sum_copy(d, a):
        slot = jnp.where(odd == 1, jnp.where(d == 1, 2, 3 - d), jnp.where(d == 1, 2, 3))
        to = jnp.where(odd == 1, b - 1, (b - d + rows) % rows)
        return remote(acc.at[d, a], arr.at[slot, a], sum_send.at[d, a], sum_recv.at[slot, a], (to, z))

    def arrived(slot, a):
        pltpu.make_async_copy(arr.at[slot, a], arr.at[slot, a], sum_recv.at[slot, a]).wait()

    def send_sum(d):
        @pl.loop(0, actions)
        def _(a):
            sum_copy(d, a).start()

    def add_and_send(d):
        @pl.loop(0, actions)
        def _(a):
            arrived(2 - d, a)
            acc[d, a] += arr[2 - d, a]
            sum_copy(d, a).start()

    @pl.loop(0, 4)
    def _(h):
        value_copy(h).wait()

    slow_end = (odd == 1) & ((z == 3) & (k < 2) | (z == 0) & (k == 2))
    own_from = jnp.where(slow_end, 24, jnp.where((b == 3) & (z == 0), half, pieces))
    in_turn = (k == 2) | (k == 1) & (z == 0)
    hops = jnp.where(z > k, z - k, k - z)
    far_from = jnp.where(hops == 0, jnp.where(k % 2 == 0, 16, 0), jnp.where(hops == 3, 6, 1 + 2 * hops))
    far_from = jnp.where((z == 0) & (b == 4) | (z == 3) & (b == 2), 7, jnp.where((z == 3) & (b == 4), 16, far_from))
    ahead = (b == 2) & (z == 0)
    far_each = jnp.where((far_from >= 14) | ahead, 4, 2)
    far_end = far_from + pieces // far_each
    hops_r = jnp.where(z > kr, z - kr, kr - z)
    relay_from = jnp.where(odd == 1, 2 * hops_r - 2, 2 * hops_r)
    end_from = jnp.where(odd == 1, jnp.where((kr == 0) | (kr == 3), 6, 4), jnp.where((kr == 0) | (kr == 3), 8, jnp.where(kr == 1, 18, 17)))

    @pl.loop(0, 2 * pieces)
    def _(g):
        @pl.when((g > 0) & (g < half - 1))
        def _():
            for i in range(2):
                value_copy(2 * g + 2 + i).wait()

        @pl.when(ahead & (g == half))
        def _():
            add_and_send(2)

        @pl.when((z == 1) & (dist[0] == 2) & (g < pieces // 4))
        def _():
            for i in range(4):
                for j in range(2):
                    direct_copy(j, 2 + j, 4 * g + i).start()

        for j in range(2):
            near_turn = jnp.where(z == 1, (g < 2) | (g >= 6), (g < half) | (g < pieces) & (g % 2 == 0) | (g >= 20))
            near_h = jnp.where(z == 1, jnp.where(g < 2, g, g - 4), jnp.where(g < half, g, jnp.where(g < pieces, half + (g - half) // 2, g - 8)))

            @pl.when(sends_near(j) & near_turn & (near_h < pieces))
            def _():
                direct_copy(j, dist[j], near_h).start()

        @pl.when((z == 1) & (dist[0] == 1) & (g == half + 1))
        def _():
            @pl.loop(0, pieces)
            def _(h):
                for j in range(2):
                    direct_copy(j, 1 + j, h).start()

        @pl.when(later & (g == 6))
        def _():
            @pl.loop(0, pieces)
            def _(h):
                for j in range(2):
                    first_copy(j, 1 + j, h).start()

        @pl.when(lifts & (g < pieces + 1) & (g != half))
        def _():
            for i in range(2):
                x, h = jnp.where(g < half, 1, 0), 2 * jnp.where(g < half, g, g - half - 1) + i
                pltpu.make_async_copy(relay.at[1 + x, h], relay.at[1 + x, h], relay_sem.at[1 + x, h]).wait()
                lift_copy(x, h).start()

        @pl.when(far_later & (g == 7))
        def _():
            @pl.loop(0, pieces)
            def _(h):
                first_copy(0, 3, h).start()

        @pl.loop(0, 8)
        def _(i):
            cross = g < pieces
            far_due = (g >= far_from) & (g < far_end) & (odd == 0) & (i < 4 + far_each)
            far_due = far_due | (odd == 1) & (g >= own_from) & (g < own_from + pieces) & (i == 4)
            middle = (k % 2 == 0) & ((g == 5) | (g == 10))
            near = (g == 0) | middle | (g >= pieces) & (g < 2 * pieces - before)
            d = jnp.where(i >= 4, 3 * (1 - odd), jnp.where(i < 2, odd, 2 + odd - jnp.where(in_turn, g // half, i - 2)))
            h = jnp.where(in_turn, 2 * (g % half) + i - 2, g)
            h = jnp.where(i >= 4, jnp.where(odd == 1, g - own_from, far_each * (g - far_from) + i - 4), h)
            h = jnp.where(i < 2, jnp.where(cross, jnp.where(g == 0, i, 1 + g // 5), g - pieces + before), h)

            @pl.when(jnp.where(i == 0, near, jnp.where(i == 1, g == 0, jnp.where(i < 4, cross, far_due))))
            def _():
                process(d, h)

        @pl.when(takes & (g >= relay_from) & (g < relay_from + half))
        def _():
            for i in range(2):
                relay_step(2 * (g - relay_from) + i)

        end_step = jnp.where(splits & (g >= 22), g - 19, jnp.where(splits & (g >= end_from + 3), 4, g - end_from))

        @pl.when(ends & (end_step >= 0) & (end_step < 4))
        def _():
            @pl.loop(0, pieces // 4)
            def _(i):
                h = pieces // 4 * end_step + i

                @pl.when(jnp.logical_not(borrows) | (h >= borrowed))
                def _():
                    end_copy(h).start()

        first_at = jnp.where(in_turn & (z != 2), half, pieces)

        @pl.when((odd == 1) & (g == first_at - 1))
        def _():
            send_sum(3)

        @pl.when((odd == 1) & (g == pieces - 1))
        def _():
            send_sum(2)

        @pl.when((odd == 1) & (g == 2 * pieces - before - 1))
        def _():
            send_sum(1)

        @pl.when((z == 3) & (k == 2) & (g == pieces - 5))
        def _():
            pl.semaphore_signal(there_sem, inc=1, device_id=(6, 3), device_id_type=MESH)

        @pl.when((z == 3) & (b == 6) & (g == pieces + 1))
        def _():
            pl.semaphore_wait(there_sem, 2)

        @pl.when((odd == 0) & jnp.logical_not(ahead) & (g == first_at + 1))
        def _():
            add_and_send(2)

        @pl.when((odd == 0) & (g == pieces + jnp.where((z == 3) & (b == 4), 4, 2)))
        def _():
            add_and_send(1)

        @pl.when((odd == 0) & (g == jnp.where((b == 0) & (z == 2) | (b == 4) & (z == 0), 20, far_end - 1)))
        def _():
            send_sum(3)

    @pl.when(slow_end)
    def _():
        @pl.loop(half, pieces)
        def _(h):
            process(0, h)

    @pl.loop(1, STEPS)
    def _(d):
        @pl.loop(0, actions)
        def _(a):
            sum_copy(d, a).wait_send()

    for j in range(2):
        every((dist[j] > 0) & (dist[j] < STEPS), lambda h: first_copy(j, dist[j], h).wait_send())
        every(sends_cross(j) | sends_near(j), lambda h: direct_copy(j, dist[j], h).wait_send())
    every(is_far, lambda h: far_copy(h).wait_send())
    every(is_aside, lambda h: aside_copy(h).wait_send())
    for d in range(1, STEPS):
        every(in_chain(d, pieces), lambda h: chain_copy(d, h).wait_send())

    @pl.loop(0, pieces)
    def _(h):
        @pl.when(in_chain(0, h))
        def _():
            chain_copy(0, h).wait_send()

        @pl.when(ends & (jnp.logical_not(borrows) | (h >= borrowed)))
        def _():
            end_copy(h).wait_send()

    every(turns, lambda h: turn_copy(h).wait_send())
    every(passes, lambda h: pass_copy(h).wait_send())
    every(hands, lambda h: hand_copy(h).wait_send())
    for x in range(2):
        every(crosses, lambda h: cross_copy(x, h).wait_send())
        every(lifts, lambda h: lift_copy(x, h).wait_send())

    for load in loads:
        load.wait()

    @pl.loop(0, actions)
    def _(a):
        arrived(2, a)
        arrived(3, a)

        @pl.loop(0, height // 16)
        def _(n):
            at = pl.ds(pl.multiple_of(n * 16, 16), 16)
            backup = e_buf[a, at, :].astype(jnp.float32) + acc[0, a, at, :] + arr[2, a, at, :] + arr[3, a, at, :]
            cost = c_buf[a, at, :].astype(jnp.float32) + DISCOUNT * backup

            @pl.when(a == 0)
            def _():
                out_ref[at, :] = cost

            @pl.when(a > 0)
            def _():
                out_ref[at, :] = jnp.minimum(out_ref[at, :], cost)


def routed(transitions, values, earlier_sum, section_costs):
    actions, height, _ = transitions.shape
    width, scenarios = values.shape
    pieces = width // CHUNK
    anywhere = pl.BlockSpec(memory_space=pl.ANY)
    dma = pltpu.SemaphoreType.DMA
    return pl.pallas_call(
        routed_kernel,
        out_shape=(
            jax.ShapeDtypeStruct((height, scenarios), jnp.float32),
            jax.ShapeDtypeStruct((3, pieces, actions, height, CHUNK), jnp.bfloat16),
        ),
        in_specs=[anywhere] * 4,
        out_specs=(pl.BlockSpec(memory_space=pltpu.VMEM), anywhere),
        scratch_shapes=[
            pltpu.VMEM((STEPS, pieces, actions, height, CHUNK), jnp.bfloat16),
            pltpu.VMEM((width, scenarios), jnp.bfloat16),
            pltpu.VMEM((STEPS, actions, height, scenarios), jnp.float32),
            pltpu.VMEM((STEPS, actions, height, scenarios), jnp.float32),
            pltpu.VMEM((actions, height, scenarios), jnp.bfloat16),
            pltpu.VMEM((actions, height, scenarios), jnp.bfloat16),
            dma((2,)),
            dma((pieces,)),
            dma((STEPS, pieces)),
            dma((3, pieces)),
            dma((2, pieces)),
            dma((2, pieces)),
            dma((2, pieces)),
            dma((STEPS, pieces)),
            dma((pieces,)),
            dma((2, pieces)),
            dma((pieces,)),
            dma((pieces,)),
            dma((2, pieces)),
            dma((STEPS, actions)),
            dma((STEPS, actions)),
            pltpu.SemaphoreType.REGULAR,
        ],
        compiler_params=pltpu.CompilerParams(
            collective_id=0, has_side_effects=True, vmem_limit_bytes=66_000_000
        ),
    )(transitions, values, earlier_sum, section_costs)[0]


def local(transitions, values, earlier_sum, section_costs):
    if lax.axis_size("row") == 8 and lax.axis_size("col") == 4:
        return routed(transitions, values, earlier_sum, section_costs)
    return general(transitions, values, earlier_sum, section_costs)


def solution(mesh):
    in_specs = (
        P(None, "row", "col"),
        P("row", "col"),
        P(None, "row", "col"),
        P(None, "row", "col"),
    )
    out_specs = P("row", "col")
    return jax.shard_map(local, mesh=mesh, in_specs=in_specs, out_specs=out_specs, check_vma=False)
```

```python
import functools

import jax
import jax.numpy as jnp
from jax import lax
from jax.experimental import pallas as pl
from jax.experimental.pallas import tpu as pltpu
from jax.sharding import PartitionSpec as P

STEPS = 4
PIECES = 8
DISCOUNT = 0.97
MESH = pl.DeviceIdType.MESH


def general_kernel(
    rows, cols, t_ref, v_ref, e_ref, c_ref, out_ref,
    slots, v_buf, work, arrived, e_buf, c_buf,
    in_sem, own_sem, slot_sem, first_sem, up_sem, down_sem, sum_send, sum_recv,
):
    b = lax.axis_index("row")
    z = lax.axis_index("col")
    ratio = rows // cols
    q = b // ratio
    actions = t_ref.shape[0]
    width = v_ref.shape[0]
    half = width // PIECES
    sums = (STEPS - 1) * actions
    total = STEPS * actions

    loads = [
        pltpu.make_async_copy(v_ref, v_buf, in_sem.at[0]),
        pltpu.make_async_copy(e_ref, e_buf, in_sem.at[1]),
        pltpu.make_async_copy(c_ref, c_buf, in_sem.at[2]),
    ]
    for load in loads:
        load.start()

    barrier = pltpu.get_barrier_semaphore()
    for d in range(1, STEPS):
        for by in (d, rows - d):
            pl.semaphore_signal(barrier, inc=1, device_id=((b + by) % rows, z), device_id_type=MESH)

    @pl.when(z > 0)
    def _():
        pl.semaphore_signal(barrier, inc=1, device_id=(b, z - 1), device_id_type=MESH)

    @pl.when(z < cols - 1)
    def _():
        pl.semaphore_signal(barrier, inc=1, device_id=(b, z + 1), device_id_type=MESH)

    beside = jnp.where(z > 0, 1, 0) + jnp.where(z < cols - 1, 1, 0)
    pl.semaphore_wait(barrier, 2 * (STEPS - 1) + beside)

    def held(j, a, h):
        offset = pl.multiple_of(j * width + h * half, 128)
        return t_ref.at[a, :, pl.ds(offset, half)]

    def first_copy(j, d, a, h):
        i = (d - 1) * actions + a
        return pltpu.make_async_remote_copy(
            src_ref=held(j, a, h), dst_ref=slots.at[i, h],
            send_sem=first_sem.at[j, a, h], recv_sem=slot_sem.at[i, h],
            device_id=(z * ratio + j, z), device_id_type=MESH,
        )

    def own_copy(j, a, h):
        i = (STEPS - 1) * actions + a
        return pltpu.make_async_copy(held(j, a, h), slots.at[i, h], own_sem.at[a, h])

    def for_blocks(away, own):
        for j in range(ratio):
            d = (z * ratio + j - b + rows) % rows

            @pl.when((d > 0) & (d < STEPS))
            def _():
                @pl.loop(0, actions)
                def _(a):
                    for h in range(PIECES):
                        away(j, d, a, h)

            if own is not None:
                @pl.when(d == 0)
                def _():
                    @pl.loop(0, actions)
                    def _(a):
                        for h in range(PIECES):
                            own(j, a, h)

    for_blocks(
        lambda j, d, a, h: first_copy(j, d, a, h).start(),
        lambda j, a, h: own_copy(j, a, h).start(),
    )

    def along(i, h, by, sem):
        return pltpu.make_async_remote_copy(
            src_ref=slots.at[i, h], dst_ref=slots.at[i, h],
            send_sem=sem.at[i, h], recv_sem=slot_sem.at[i, h],
            device_id=(b, z + by), device_id_type=MESH,
        )

    goes_up = (z >= q) & (z < cols - 1)
    goes_down = (z <= q) & (z > 0)

    def sum_copy(i):
        d = i // actions + 1
        return pltpu.make_async_remote_copy(
            src_ref=work.at[i], dst_ref=arrived.at[i],
            send_sem=sum_send.at[i], recv_sem=sum_recv.at[i],
            device_id=((b - d + rows) % rows, z), device_id_type=MESH,
        )

    def finish(a):
        for d in range(STEPS - 1):
            sum_copy(d * actions + a).wait_recv()

        @pl.loop(0, out_ref.shape[0] // 16)
        def _(k):
            at = pl.ds(pl.multiple_of(k * 16, 16), 16)
            backup = e_buf[a, at, :].astype(jnp.float32) + work[sums + a, at, :]
            for d in range(STEPS - 1):
                backup = backup + arrived[d * actions + a, at, :]
            cost = c_buf[a, at, :].astype(jnp.float32) + DISCOUNT * backup

            @pl.when(a == 0)
            def _():
                out_ref[at, :] = cost

            @pl.when(a > 0)
            def _():
                out_ref[at, :] = jnp.minimum(out_ref[at, :], cost)

    @pl.loop(0, total)
    def _(i):
        for h in range(PIECES):
            local = (i >= sums) & (z == q)

            @pl.when(local)
            def _():
                own_copy(b % ratio, i % actions, h).wait()

            @pl.when(jnp.logical_not(local))
            def _():
                along(i, h, 0, up_sem).wait_recv()

            @pl.when(goes_up)
            def _():
                along(i, h, 1, up_sem).start()

            @pl.when(goes_down)
            def _():
                along(i, h, -1, down_sem).start()

            if h == 0:
                @pl.when(i == 0)
                def _():
                    for load in loads:
                        load.wait()

            tile = 512

            @pl.loop(0, work.shape[2] // tile)
            def _(n):
                at = pl.ds(pl.multiple_of(n * tile, tile), tile)
                product = jnp.dot(
                    slots[i, h], v_buf[h * half:(h + 1) * half, at],
                    preferred_element_type=jnp.float32,
                )
                if h == 0:
                    work[i, :, at] = product
                else:
                    work[i, :, at] += product

        @pl.when((i >= 1) & (i <= sums))
        def _():
            sum_copy(i - 1).start()

        @pl.when(i > sums)
        def _():
            finish(i - 1 - sums)

    finish(actions - 1)

    @pl.loop(0, sums)
    def _(i):
        sum_copy(i).wait_send()

    for_blocks(lambda j, d, a, h: first_copy(j, d, a, h).wait_send(), None)

    @pl.when(goes_up)
    def _():
        @pl.loop(0, total)
        def _(i):
            for h in range(PIECES):
                along(i, h, 1, up_sem).wait_send()

    @pl.when(goes_down)
    def _():
        @pl.loop(0, total)
        def _(i):
            for h in range(PIECES):
                along(i, h, -1, down_sem).wait_send()


def general(transitions, values, earlier_sum, section_costs):
    rows = lax.axis_size("row")
    cols = lax.axis_size("col")
    actions, height, _ = transitions.shape
    width, scenarios = values.shape
    total = STEPS * actions
    sums = (STEPS - 1) * actions
    ratio = rows // cols
    anywhere = pl.BlockSpec(memory_space=pl.ANY)
    dma = pltpu.SemaphoreType.DMA
    return pl.pallas_call(
        functools.partial(general_kernel, rows, cols),
        out_shape=jax.ShapeDtypeStruct((height, scenarios), jnp.float32),
        in_specs=[anywhere] * 4,
        out_specs=pl.BlockSpec(memory_space=pltpu.VMEM),
        scratch_shapes=[
            pltpu.VMEM((total, PIECES, height, width // PIECES), jnp.bfloat16),
            pltpu.VMEM((width, scenarios), jnp.bfloat16),
            pltpu.VMEM((total, height, scenarios), jnp.float32),
            pltpu.VMEM((sums, height, scenarios), jnp.float32),
            pltpu.VMEM((actions, height, scenarios), jnp.bfloat16),
            pltpu.VMEM((actions, height, scenarios), jnp.bfloat16),
            dma((3,)),
            dma((actions, PIECES)),
            dma((total, PIECES)),
            dma((ratio, actions, PIECES)),
            dma((total, PIECES)),
            dma((total, PIECES)),
            dma((sums,)),
            dma((sums,)),
        ],
        compiler_params=pltpu.CompilerParams(
            collective_id=0, has_side_effects=True, vmem_limit_bytes=66_000_000
        ),
    )(transitions, values, earlier_sum, section_costs)


CHUNK = 256
LENT = (2, 6)
ACROSS = (
    ((2, 0), (1, 1)), ((2, 0), (0, 1)), ((3, 0), (2, 1)), ((3, 0), (1, 1)), ((3, 0), (0, 1)),
    ((5, 3), (4, 2)), ((4, 3), (6, 2)), ((5, 3), (7, 2)),
    ((0, 3), (5, 2)), ((1, 3), (4, 2)), ((2, 3), (7, 2)), ((3, 3), (6, 2)),
    ((4, 0), (1, 1)), ((5, 0), (0, 1)), ((6, 0), (3, 1)), ((7, 0), (2, 1)),
)


def routed_kernel(
    t_ref, v_ref, e_ref, c_ref, out_ref, relay,
    slots, v_buf, acc, arr, e_buf, c_buf,
    in_sem, value_sem, slot_sem, relay_sem, first_sem, direct_sem, alt_sem, fwd_sem, minor_sem, disp_sem,
    relay_z_sem, relay_in_sem, relay_x_sem, sum_send, sum_recv, there_sem,
):
    b = lax.axis_index("row")
    z = lax.axis_index("col")
    rows = 8
    k = b // 2
    odd = b % 2
    actions, height, _ = t_ref.shape
    width, scenarios = v_ref.shape
    pieces = width // CHUNK
    half = pieces // 2

    def every(condition, do):
        @pl.when(condition)
        def _():
            @pl.loop(0, pieces)
            def _(h):
                do(h)

    def held(j, h):
        return t_ref.at[:, :, pl.ds(pl.multiple_of(j * width + h * CHUNK, 128), CHUNK)]

    def own_copy(j, h):
        return pltpu.make_async_copy(held(j, h), slots.at[0, h], slot_sem.at[0, h])

    dist = [(2 * z + j - b + rows) % rows for j in range(2)]
    barrier = pltpu.get_barrier_semaphore()
    for by in range(1, rows):
        pl.semaphore_signal(barrier, inc=1, device_id=((b + by) % rows, z), device_id_type=MESH)

    @pl.when(z > 0)
    def _():
        pl.semaphore_signal(barrier, inc=1, device_id=(b, z - 1), device_id_type=MESH)

    @pl.when(z < 3)
    def _():
        pl.semaphore_signal(barrier, inc=1, device_id=(b, z + 1), device_id_type=MESH)

    greeted = rows - 1 + jnp.where(z > 0, 1, 0) + jnp.where(z < 3, 1, 0)
    for (to, by) in ACROSS:
        @pl.when((b == to[0]) & (z == to[1]))
        def _():
            pl.semaphore_signal(barrier, inc=1, device_id=by, device_id_type=MESH)

        greeted = greeted + jnp.where((b == by[0]) & (z == by[1]), 1, 0)

    def value_copy(h):
        at = pl.ds(pl.multiple_of(h * CHUNK, CHUNK), CHUNK)
        return pltpu.make_async_copy(v_ref.at[at], v_buf.at[at], value_sem.at[h])

    @pl.loop(0, 4)
    def _(h):
        value_copy(h).start()

    for j in range(2):
        every(dist[j] == 0, lambda h: own_copy(j, h).start())

    @pl.loop(4, pieces)
    def _(h):
        value_copy(h).start()

    loads = [
        pltpu.make_async_copy(e_ref, e_buf, in_sem.at[0]),
        pltpu.make_async_copy(c_ref, c_buf, in_sem.at[1]),
    ]
    for load in loads:
        load.start()

    pl.semaphore_wait(barrier, greeted)

    def remote(src, dst, send, recv, to):
        return pltpu.make_async_remote_copy(
            src_ref=src, dst_ref=dst, send_sem=send, recv_sem=recv, device_id=to, device_id_type=MESH
        )

    way = jnp.where(k < 2, 1, -1)
    chained = (k < 2) & (z >= k) & (z < 3) | (k >= 2) & (z <= k) & (z > 0)
    starts = chained & (z == k) & (odd == 0)
    before = jnp.where(k % 2 == 0, 4, 2)

    @pl.when(starts)
    def _():
        @pl.loop(0, before)
        def _(h):
            remote(held(0, h), slots.at[0, h], fwd_sem.at[0, h], slot_sem.at[0, h], (b, z + way)).start()

    side = jnp.where(z < 2, 1, -1)

    def first_copy(j, d, h):
        return remote(held(j, h), slots.at[d, h], first_sem.at[j, h], slot_sem.at[d, h], (2 * z + j, z))

    def direct_copy(j, d, h):
        to = jnp.where(z == 1, 0, 3)
        return remote(held(j, h), slots.at[d, h], direct_sem.at[j, h], slot_sem.at[d, h], (2 * z + j, to))

    def far_copy(h):
        return remote(held(0, h), relay.at[0, h], alt_sem.at[0, h], relay_sem.at[0, h], (b, z + side))

    def aside_copy(h):
        return remote(held(1, h), relay.at[0, h], alt_sem.at[1, h], relay_sem.at[0, h], ((b + 3) % rows, z))

    is_far = dist[0] == 3
    is_aside = dist[1] == 0

    def sends_cross(j):
        return (z == 1) & (dist[j] > j) & (dist[j] <= 2 + j)

    def sends_near(j):
        return ((z == 1) | (z == 2)) & (dist[j] <= j)

    far_later = is_far & (z % 2 == 0)
    later = (z == 2) & (dist[0] == 1)

    def first_both(h):
        for j in range(2):
            first_copy(j, dist[j], h).start()

    firsts = [(dist[j] > 0) & (dist[j] <= 2 + j) & jnp.logical_not(later) for j in range(2)]
    every(firsts[0] & firsts[1], first_both)
    every(firsts[0] & jnp.logical_not(firsts[1]), lambda h: first_copy(0, dist[0], h).start())
    every(firsts[1] & jnp.logical_not(firsts[0]), lambda h: first_copy(1, dist[1], h).start())
    every(is_far, lambda h: far_copy(h).start())
    every(is_far & jnp.logical_not(far_later), lambda h: first_copy(0, 3, h).start())
    every(is_aside, lambda h: aside_copy(h).start())

    turns = (odd == 0) & (z == k) & ((k == 1) | (k == 2))
    crosses = (z == 2) & (k == 2)

    def chain_copy(d, h):
        return remote(slots.at[d, h], slots.at[d, h], fwd_sem.at[d, h], slot_sem.at[d, h], (b, z + way))

    lends = ((b == 1) | (b == 3)) & (z == 2)
    lent = jnp.where(k == 0, LENT[0], LENT[1])

    def in_chain(d, h):
        return chained & (d < 3 + odd) & (d >= odd) | lends & (d == 0) & (h < lent)

    def turn_copy(h):
        return remote(slots.at[3, h], slots.at[3, h], minor_sem.at[h], slot_sem.at[3, h], (b, z - way))

    def cross_copy(x, h):
        return remote(
            slots.at[1 + odd + x, h], relay.at[1 + x, h], disp_sem.at[x, h], relay_sem.at[1 + x, h], (b + 2, z)
        )

    def is_cross(d):
        return crosses & (d > odd) & (d <= 2 + odd)

    kr = (b // 2 + 2) % 4
    br = jnp.where(odd == 1, (b + 3) % rows, (b + 5) % rows)
    dr = jnp.where(odd == 1, 3, 0)
    way_r = jnp.where(kr < 2, 1, -1)
    relays = (kr < 2) & (z >= kr) | (kr >= 2) & (z <= kr)
    takes = relays & ((z != kr) | (odd == 0)) & (z + way_r >= 0) & (z + way_r <= 3)
    ends = takes & ((z + way_r == 0) | (z + way_r == 3))
    passes = takes & jnp.logical_not(ends)
    borrows = ((b == 4) | (b == 6)) & (z == 2)
    borrowed = jnp.where(k == 2, LENT[0], LENT[1])
    splits = (b == 4) & (z == 2)
    hands = takes & (z != kr)
    lifts = (z == 2) & (k == 3)

    def pass_copy(h):
        return remote(relay.at[0, h], relay.at[0, h], relay_z_sem.at[h], relay_sem.at[0, h], (b, z + way_r))

    def end_copy(h):
        return remote(
            relay.at[0, h], slots.at[dr, h], relay_z_sem.at[h], slot_sem.at[dr, h], (br, z + way_r)
        )

    def hand_copy(h):
        return remote(relay.at[0, h], slots.at[dr, h], relay_in_sem.at[h], slot_sem.at[dr, h], (br, z))

    def lift_copy(x, h):
        d = 1 + odd + x
        return remote(relay.at[1 + x, h], slots.at[d, h], relay_x_sem.at[x, h], slot_sem.at[d, h], ((b + 6) % rows, 3))

    def relay_step(h):
        pltpu.make_async_copy(relay.at[0, h], relay.at[0, h], relay_sem.at[0, h]).wait()

        @pl.when(passes)
        def _():
            pass_copy(h).start()

        @pl.when(hands)
        def _():
            hand_copy(h).start()

    def process(d, h):
        pltpu.make_async_copy(slots.at[d, h], slots.at[d, h], slot_sem.at[d, h]).wait()

        @pl.when(in_chain(d, h) & jnp.logical_not(starts & (d == 0) & (h < before)))
        def _():
            chain_copy(d, h).start()

        @pl.when(turns & (d == 3))
        def _():
            turn_copy(h).start()

        @pl.when(is_cross(d))
        def _():
            cross_copy(d - 1 - odd, h).start()

        tile = 1536

        @pl.loop(0, scenarios // tile)
        def _(n):
            at = pl.ds(pl.multiple_of(n * tile, tile), tile)
            rows_at = pl.ds(pl.multiple_of(h * CHUNK, CHUNK), CHUNK)
            product = jnp.dot(
                slots[d, h].reshape(actions * height, CHUNK), v_buf[rows_at, at],
                preferred_element_type=jnp.float32,
            )
            product = product.reshape(actions, height, tile)
            acc[d, :, :, at] = jnp.where(h == 0, product, acc[d, :, :, at] + product)

    def sum_copy(d, a):
        slot = jnp.where(odd == 1, jnp.where(d == 1, 2, 3 - d), jnp.where(d == 1, 2, 3))
        to = jnp.where(odd == 1, b - 1, (b - d + rows) % rows)
        return remote(acc.at[d, a], arr.at[slot, a], sum_send.at[d, a], sum_recv.at[slot, a], (to, z))

    def arrived(slot, a):
        pltpu.make_async_copy(arr.at[slot, a], arr.at[slot, a], sum_recv.at[slot, a]).wait()

    def send_sum(d):
        @pl.loop(0, actions)
        def _(a):
            sum_copy(d, a).start()

    def add_and_send(d):
        @pl.loop(0, actions)
        def _(a):
            arrived(2 - d, a)
            acc[d, a] += arr[2 - d, a]
            sum_copy(d, a).start()

    @pl.loop(0, 4)
    def _(h):
        value_copy(h).wait()

    slow_end = (odd == 1) & ((z == 3) & (k < 2) | (z == 0) & (k == 2))
    own_from = jnp.where(slow_end, 24, jnp.where((b == 3) & (z == 0), half, pieces))
    in_turn = (k == 2) | (k == 1) & (z == 0)
    hops = jnp.where(z > k, z - k, k - z)
    far_from = jnp.where(hops == 0, jnp.where(k % 2 == 0, 16, 0), jnp.where(hops == 3, 6, 1 + 2 * hops))
    far_from = jnp.where((z == 0) & (b == 4) | (z == 3) & (b == 2), 7, jnp.where((z == 3) & (b == 4), 16, far_from))
    ahead = (b == 2) & (z == 0)
    far_each = jnp.where((far_from >= 14) | ahead, 4, 2)
    far_end = far_from + pieces // far_each
    hops_r = jnp.where(z > kr, z - kr, kr - z)
    relay_from = jnp.where(odd == 1, 2 * hops_r - 2, 2 * hops_r)
    end_from = jnp.where(odd == 1, jnp.where((kr == 0) | (kr == 3), 6, 4), jnp.where((kr == 0) | (kr == 3), 8, jnp.where(kr == 1, 18, 17)))

    @pl.loop(0, 2 * pieces)
    def _(g):
        @pl.when((g > 0) & (g < half - 1))
        def _():
            for i in range(2):
                value_copy(2 * g + 2 + i).wait()

        @pl.when(ahead & (g == half))
        def _():
            add_and_send(2)

        @pl.when((z == 1) & (dist[0] == 2) & (g < pieces // 4))
        def _():
            for i in range(4):
                for j in range(2):
                    direct_copy(j, 2 + j, 4 * g + i).start()

        for j in range(2):
            near_turn = jnp.where(z == 1, (g < 2) | (g >= 6), (g < half) | (g < pieces) & (g % 2 == 0) | (g >= 20))
            near_h = jnp.where(z == 1, jnp.where(g < 2, g, g - 4), jnp.where(g < half, g, jnp.where(g < pieces, half + (g - half) // 2, g - 8)))

            @pl.when(sends_near(j) & near_turn & (near_h < pieces))
            def _():
                direct_copy(j, dist[j], near_h).start()

        @pl.when((z == 1) & (dist[0] == 1) & (g == half + 1))
        def _():
            @pl.loop(0, pieces)
            def _(h):
                for j in range(2):
                    direct_copy(j, 1 + j, h).start()

        @pl.when(later & (g == 6))
        def _():
            @pl.loop(0, pieces)
            def _(h):
                for j in range(2):
                    first_copy(j, 1 + j, h).start()

        @pl.when(lifts & (g < pieces + 1) & (g != half))
        def _():
            for i in range(2):
                x, h = jnp.where(g < half, 1, 0), 2 * jnp.where(g < half, g, g - half - 1) + i
                pltpu.make_async_copy(relay.at[1 + x, h], relay.at[1 + x, h], relay_sem.at[1 + x, h]).wait()
                lift_copy(x, h).start()

        @pl.when(far_later & (g == 7))
        def _():
            @pl.loop(0, pieces)
            def _(h):
                first_copy(0, 3, h).start()

        @pl.loop(0, 8)
        def _(i):
            cross = g < pieces
            far_due = (g >= far_from) & (g < far_end) & (odd == 0) & (i < 4 + far_each)
            far_due = far_due | (odd == 1) & (g >= own_from) & (g < own_from + pieces) & (i == 4)
            middle = (k % 2 == 0) & ((g == 5) | (g == 10))
            near = (g == 0) | middle | (g >= pieces) & (g < 2 * pieces - before)
            d = jnp.where(i >= 4, 3 * (1 - odd), jnp.where(i < 2, odd, 2 + odd - jnp.where(in_turn, g // half, i - 2)))
            h = jnp.where(in_turn, 2 * (g % half) + i - 2, g)
            h = jnp.where(i >= 4, jnp.where(odd == 1, g - own_from, far_each * (g - far_from) + i - 4), h)
            h = jnp.where(i < 2, jnp.where(cross, jnp.where(g == 0, i, 1 + g // 5), g - pieces + before), h)

            @pl.when(jnp.where(i == 0, near, jnp.where(i == 1, g == 0, jnp.where(i < 4, cross, far_due))))
            def _():
                process(d, h)

        @pl.when(takes & (g >= relay_from) & (g < relay_from + half))
        def _():
            for i in range(2):
                relay_step(2 * (g - relay_from) + i)

        end_step = jnp.where(splits & (g >= 22), g - 19, jnp.where(splits & (g >= end_from + 3), 4, g - end_from))

        @pl.when(ends & (end_step >= 0) & (end_step < 4))
        def _():
            @pl.loop(0, pieces // 4)
            def _(i):
                h = pieces // 4 * end_step + i

                @pl.when(jnp.logical_not(borrows) | (h >= borrowed))
                def _():
                    end_copy(h).start()

        first_at = jnp.where(in_turn & (z != 2), half, pieces)

        @pl.when((odd == 1) & (g == first_at - 1))
        def _():
            send_sum(3)

        @pl.when((odd == 1) & (g == pieces - 1))
        def _():
            send_sum(2)

        @pl.when((odd == 1) & (g == 2 * pieces - before - 1))
        def _():
            send_sum(1)

        @pl.when((z == 3) & (k == 2) & (g == pieces - 5))
        def _():
            pl.semaphore_signal(there_sem, inc=1, device_id=(6, 3), device_id_type=MESH)

        @pl.when((z == 3) & (b == 6) & (g == pieces + 1))
        def _():
            pl.semaphore_wait(there_sem, 2)

        @pl.when((odd == 0) & jnp.logical_not(ahead) & (g == first_at + 1))
        def _():
            add_and_send(2)

        @pl.when((odd == 0) & (g == pieces + jnp.where((z == 3) & (b == 4), 4, 2)))
        def _():
            add_and_send(1)

        @pl.when((odd == 0) & (g == jnp.where((b == 0) & (z == 2) | (b == 4) & (z == 0), 20, far_end - 1)))
        def _():
            send_sum(3)

    @pl.when(slow_end)
    def _():
        @pl.loop(half, pieces)
        def _(h):
            process(0, h)

    @pl.loop(1, STEPS)
    def _(d):
        @pl.loop(0, actions)
        def _(a):
            sum_copy(d, a).wait_send()

    for j in range(2):
        every((dist[j] > 0) & (dist[j] < STEPS), lambda h: first_copy(j, dist[j], h).wait_send())
        every(sends_cross(j) | sends_near(j), lambda h: direct_copy(j, dist[j], h).wait_send())
    every(is_far, lambda h: far_copy(h).wait_send())
    every(is_aside, lambda h: aside_copy(h).wait_send())
    for d in range(1, STEPS):
        every(in_chain(d, pieces), lambda h: chain_copy(d, h).wait_send())

    @pl.loop(0, pieces)
    def _(h):
        @pl.when(in_chain(0, h))
        def _():
            chain_copy(0, h).wait_send()

        @pl.when(ends & (jnp.logical_not(borrows) | (h >= borrowed)))
        def _():
            end_copy(h).wait_send()

    every(turns, lambda h: turn_copy(h).wait_send())
    every(passes, lambda h: pass_copy(h).wait_send())
    every(hands, lambda h: hand_copy(h).wait_send())
    for x in range(2):
        every(crosses, lambda h: cross_copy(x, h).wait_send())
        every(lifts, lambda h: lift_copy(x, h).wait_send())

    for load in loads:
        load.wait()

    @pl.loop(0, actions)
    def _(a):
        arrived(2, a)
        arrived(3, a)

        @pl.loop(0, height // 16)
        def _(n):
            at = pl.ds(pl.multiple_of(n * 16, 16), 16)
            backup = e_buf[a, at, :].astype(jnp.float32) + acc[0, a, at, :] + arr[2, a, at, :] + arr[3, a, at, :]
            cost = c_buf[a, at, :].astype(jnp.float32) + DISCOUNT * backup

            @pl.when(a == 0)
            def _():
                out_ref[at, :] = cost

            @pl.when(a > 0)
            def _():
                out_ref[at, :] = jnp.minimum(out_ref[at, :], cost)


def routed(transitions, values, earlier_sum, section_costs):
    actions, height, _ = transitions.shape
    width, scenarios = values.shape
    pieces = width // CHUNK
    anywhere = pl.BlockSpec(memory_space=pl.ANY)
    dma = pltpu.SemaphoreType.DMA
    return pl.pallas_call(
        routed_kernel,
        out_shape=(
            jax.ShapeDtypeStruct((height, scenarios), jnp.float32),
            jax.ShapeDtypeStruct((3, pieces, actions, height, CHUNK), jnp.bfloat16),
        ),
        in_specs=[anywhere] * 4,
        out_specs=(pl.BlockSpec(memory_space=pltpu.VMEM), anywhere),
        scratch_shapes=[
            pltpu.VMEM((STEPS, pieces, actions, height, CHUNK), jnp.bfloat16),
            pltpu.VMEM((width, scenarios), jnp.bfloat16),
            pltpu.VMEM((STEPS, actions, height, scenarios), jnp.float32),
            pltpu.VMEM((STEPS, actions, height, scenarios), jnp.float32),
            pltpu.VMEM((actions, height, scenarios), jnp.bfloat16),
            pltpu.VMEM((actions, height, scenarios), jnp.bfloat16),
            dma((2,)),
            dma((pieces,)),
            dma((STEPS, pieces)),
            dma((3, pieces)),
            dma((2, pieces)),
            dma((2, pieces)),
            dma((2, pieces)),
            dma((STEPS, pieces)),
            dma((pieces,)),
            dma((2, pieces)),
            dma((pieces,)),
            dma((pieces,)),
            dma((2, pieces)),
            dma((STEPS, actions)),
            dma((STEPS, actions)),
            pltpu.SemaphoreType.REGULAR,
        ],
        compiler_params=pltpu.CompilerParams(
            collective_id=0, has_side_effects=True, vmem_limit_bytes=66_000_000
        ),
    )(transitions, values, earlier_sum, section_costs)[0]


def local(transitions, values, earlier_sum, section_costs):
    if lax.axis_size("row") == 8 and lax.axis_size("col") == 4:
        return routed(transitions, values, earlier_sum, section_costs)
    return general(transitions, values, earlier_sum, section_costs)


def solution(mesh):
    in_specs = (
        P(None, "row", "col"),
        P("row", "col"),
        P(None, "row", "col"),
        P(None, "row", "col"),
    )
    out_specs = P("row", "col")
    return jax.shard_map(local, mesh=mesh, in_specs=in_specs, out_specs=out_specs, check_vma=False)
```
